128 devices in a mesh: wide: 16 (over z, x_lo, core), tall: 8 (over x_hi, y).
Axes of the slice: x: 4 (x_hi: 2, x_lo: 2; x = x_hi * 2 + x_lo), y: 4, z: 4, core: 2. Of those that a mesh axis runs over, the one named last changes fastest.
Arguments:
- initial: float32 [16384, 16384], P(('wide', 'tall')), as said below
- child_tiles: float32 [8192, 128, 128], P(('wide', 'tall')), may hold values from -0.75 to 0.75
- child_targets: int32 [8192, 2], P(('wide', 'tall')), may hold values from 0 to 127, as said below
Outputs:
- front: float32 [16384, 16384], P('tall', 'wide')
The draws below stay inside these ranges and needn't reach their ends.
Inputs may be any that keep to these rules, and one draw needn't show every extreme that they name: initial is symmetric, and assembled with its lower triangle mirrored is positive definite. `child_targets`: tile t * 8 + k of a device (t < 8, k < 8) lands on a block whose rows lie in the 128 rows of initial held by device g * 8 + t, g being the sender's index along wide; such a block's grid owner is the device at tall index (block row * 1) mod 8 and wide index (block column * 128 // 512) mod 16; the 8 tiles of one device with the same t go to 8 different grid owners, so one device sends at most one tile to one owner; in every grid row some owner gets one tile from every device.
All inputs are finite; a program needn't handle non-finite values.
Results may differ from the reference program's by a relative error of at most 0.0003.
Values sent between devices are 32-bit elements; how exact they have to be, the bound alone decides.
A program may use at most 192 MiB of HBM per device.

```python
import jax
import jax.numpy as jnp
from jax import lax

F = 16384
PANEL = 512
CH = 128
PANELS = 2
K = 8
CT = 64
ROWB = 128
N_WIDE = 16
N_TALL = 8
DEVICES = 128


def draw_initial(key, part):
    key_point, key_noise, key_diag = jax.random.split(jax.random.fold_in(key, 5), 3)
    points = jax.random.uniform(key_point, (3, F), jnp.float32, 0.0, 1.0)
    noise = jnp.clip(jax.random.normal(key_noise, (F, F), jnp.float32), -3.0, 3.0) * 0.25
    distance_sq = (points[0][:, None] - points[0][None, :]) ** 2
    distance_sq = distance_sq + (points[1][:, None] - points[1][None, :]) ** 2
    distance_sq = distance_sq + (points[2][:, None] - points[2][None, :]) ** 2
    kernel = jnp.exp(-jnp.sqrt(distance_sq) / 0.35)
    mirrored = (noise + noise.T) * 0.70710678
    root_order = jnp.sqrt(jnp.float32(F))
    lanes = jnp.arange(F, dtype=jnp.int32)
    diagonal = jax.random.uniform(key_diag, (F,), jnp.float32, 2.0, 4.0) * root_order
    matrix = 4.0 * root_order * kernel + jnp.where(lanes[:, None] == lanes[None, :], diagonal[:, None], mirrored)
    return matrix


def draw_child_targets(key, part):
    key_hot, key_score, key_row, key_tile, key_inner = jax.random.split(jax.random.fold_in(key, 11), 5)
    hot_wide = jax.random.randint(key_hot, (N_TALL,), 0, N_WIDE)
    hot_wide = hot_wide.at[N_TALL - 1].set(N_WIDE - 1)
    scores = jax.random.randint(key_score, (DEVICES, N_TALL, N_WIDE), 0, 65536)
    lanes = jnp.arange(N_WIDE, dtype=jnp.int32)
    scores = jnp.where(lanes[None, None, :] == hot_wide[None, :, None], 131072, scores)
    scores = scores * N_WIDE + lanes[None, None, :]
    best_scores, chosen = lax.top_k(scores, K)
    chosen = jnp.sort(chosen.astype(jnp.int32), axis=-1)
    devices = jnp.arange(DEVICES, dtype=jnp.int32)[:, None, None]
    talls = jnp.arange(N_TALL, dtype=jnp.int32)[None, :, None]
    owner_row = devices // N_TALL * N_TALL + talls
    row_blocks = ROWB // CH
    row_pick = jax.random.randint(key_row, (DEVICES, N_TALL, K), 0, row_blocks)
    row_pick = row_pick.at[DEVICES - 1, N_TALL - 1, K - 1].set(row_blocks - 1)
    row_pick = row_pick.at[0, 0, 0].set(0)
    block_row = owner_row * row_blocks + row_pick
    tile_at = jax.random.randint(key_tile, (DEVICES, N_TALL, K), 0, F // (PANEL * N_WIDE))
    tile_at = tile_at.at[DEVICES - 1, N_TALL - 1, K - 1].set(F // (PANEL * N_WIDE) - 1)
    inner_at = jax.random.randint(key_inner, (DEVICES, N_TALL, K), 0, PANEL // CH)
    inner_at = inner_at.at[DEVICES - 1, N_TALL - 1, K - 1].set(PANEL // CH - 1)
    block_col = (tile_at * N_WIDE + chosen) * (PANEL // CH) + inner_at
    return jnp.stack([block_row, block_col], axis=-1).reshape(DEVICES * CT, 2).astype(jnp.int32)


def steps_of(key, dims, pieces, smallest, top_value):
    loudness = 1.0
    for axis_at, parts in pieces:
        steps = jax.random.uniform(jax.random.fold_in(jax.random.fold_in(key, 6), axis_at), (parts,), jnp.float32, smallest / len(pieces), top_value / len(pieces))
        loudness = loudness * jnp.repeat(jnp.exp(steps), dims[axis_at] // parts).reshape((-1,) + (1,) * (len(dims) - 1 - axis_at))
    return loudness


def normal_values(own_key, dims, scale, limit, cuts=(), kind=jnp.bfloat16):
    level = steps_of(own_key, dims, cuts, -0.22, 0.18) if cuts else 1.0
    entries = jax.random.normal(own_key, dims, jnp.float32) * scale * level
    return jnp.minimum(jnp.maximum(entries, -limit), limit).astype(kind)


def setup_inputs(seed: int = 0) -> dict:
    keys = jax.random.split(jax.random.key(seed), 4)
    initial = draw_initial(jax.random.fold_in(keys[3], 71), 0)
    child_tiles = normal_values(keys[1], (DEVICES * CT, CH, CH), 0.25, 0.75, ((0, 128),), jnp.float32)
    child_targets = draw_child_targets(jax.random.fold_in(keys[3], 71), 0)
    return {"initial": initial, "child_tiles": child_tiles, "child_targets": child_targets}


full_precision = lax.Precision.HIGHEST

def reference(initial, child_tiles, child_targets):
    front_order = initial.shape[0]
    offsets = jnp.arange(CH, dtype=jnp.int32)
    row_index = (child_targets[:, 0] * CH)[:, None, None] + offsets[None, :, None]
    col_index = (child_targets[:, 1] * CH)[:, None, None] + offsets[None, None, :]
    matrix = initial.at[row_index, col_index].add(child_tiles)
    identity = jnp.eye(PANEL, dtype=jnp.float32)
    for panel_at in range(PANELS):
        low_row = panel_at * PANEL
        high_row = low_row + PANEL
        diag_block = matrix[low_row:high_row, low_row:high_row]
        factor = jnp.linalg.cholesky(jnp.tril(diag_block) + jnp.tril(diag_block, -1).T)
        inverse = lax.linalg.triangular_solve(factor, identity, left_side=True, lower=True)
        solved = jnp.dot(matrix[high_row:, low_row:high_row].astype(jnp.float32), inverse.T.astype(jnp.float32), precision=full_precision, preferred_element_type=jnp.float32)
        matrix = matrix.at[low_row:high_row, low_row:high_row].set(jnp.tril(factor) + jnp.triu(diag_block, 1))
        matrix = matrix.at[high_row:, low_row:high_row].set(solved)
        change = jnp.dot(solved.astype(jnp.float32), solved.T.astype(jnp.float32), precision=full_precision, preferred_element_type=jnp.float32)
        matrix = matrix.at[high_row:, high_row:].add(-change)
    tall_rows = front_order // N_TALL
    wide_cols = front_order // N_WIDE
    matrix = matrix.reshape(tall_rows // ROWB, N_TALL, ROWB, front_order).transpose(1, 0, 2, 3).reshape(front_order, front_order)
    matrix = matrix.reshape(front_order, wide_cols // PANEL, N_WIDE, PANEL).transpose(0, 2, 1, 3).reshape(front_order, front_order)
    return matrix
```

```python
import functools

import jax
import jax.numpy as jnp
from jax import lax
from jax.experimental import pallas as pl
from jax.experimental.pallas import tpu as pltpu
from jax.sharding import PartitionSpec as P

PANEL = 512
LEAD = 1024
B = 128
MESH = pl.DeviceIdType.MESH
NT = (((1,), (1,)), ((), ()))
NN = (((1,), (0,)), ((), ()))
VMEM_LIMIT = 60 * 1024 * 1024
F32 = jnp.float32


def vmem_spec():
    return pl.BlockSpec(memory_space=pltpu.VMEM)


def any_spec():
    return pl.BlockSpec(memory_space=pl.ANY)


def params(**more):
    return pltpu.CompilerParams(vmem_limit_bytes=VMEM_LIMIT, **more)


def add_kernel(cols_ref, initial_ref, tiles_ref, out_ref, strip_ref, acc, tiles, sem_in, sem_tile, sem_out, sem_strip):
    wides = acc.shape[0]
    halves = acc.shape[2] // PANEL
    count = tiles.shape[0]
    loads = []
    for q in range(halves):
        for w in range(wides):
            at = (q * wides + w) * PANEL
            loads.append(
                pltpu.make_async_copy(
                    initial_ref.at[:, at : at + PANEL],
                    acc.at[w, :, q * PANEL : (q + 1) * PANEL],
                    sem_in.at[q * wides + w],
                )
            )
    tile_load = pltpu.make_async_copy(tiles_ref, tiles, sem_tile)
    for load in loads:
        load.start()
    tile_load.start()
    for load in loads:
        load.wait()
    tile_load.wait()
    per_panel = PANEL // B

    def add(n, carry):
        col = cols_ref[n]
        block = col // per_panel
        at = pl.multiple_of((block // wides) * PANEL + (col % per_panel) * B, B)
        acc[block % wides, :, pl.ds(at, B)] += tiles[n]
        return carry

    lax.fori_loop(0, count, add, 0)
    stores = [
        pltpu.make_async_copy(acc.at[0, :, 0:PANEL], strip_ref.at[:, 0:PANEL], sem_strip.at[0]),
        pltpu.make_async_copy(acc.at[1, :, 0:PANEL], strip_ref.at[:, PANEL:LEAD], sem_strip.at[1]),
    ]
    for w in range(wides):
        stores.append(pltpu.make_async_copy(acc.at[w], out_ref.at[w], sem_out.at[w]))
    for store in stores:
        store.start()
    for store in stores:
        store.wait()


def add_tiles(initial, tiles, cols, wides):
    rows, order = initial.shape
    count = tiles.shape[0]
    width = order // wides
    return pl.pallas_call(
        add_kernel,
        grid_spec=pltpu.PrefetchScalarGridSpec(
            num_scalar_prefetch=1,
            grid=(1,),
            in_specs=[any_spec(), any_spec()],
            out_specs=[any_spec(), any_spec()],
            scratch_shapes=[
                pltpu.VMEM((wides, rows, width), F32),
                pltpu.VMEM((count, B, B), F32),
                pltpu.SemaphoreType.DMA((order // PANEL,)),
                pltpu.SemaphoreType.DMA,
                pltpu.SemaphoreType.DMA((wides,)),
                pltpu.SemaphoreType.DMA((2,)),
            ],
        ),
        out_shape=[
            jax.ShapeDtypeStruct((wides, rows, width), F32),
            jax.ShapeDtypeStruct((rows, LEAD), F32),
        ],
        compiler_params=params(),
        name="add_tiles",
    )(cols, initial, tiles)


def place():
    w = lax.axis_index("wide")
    t = lax.axis_index("tall")
    z, x, c = w // 4, (w // 2) % 2, w % 2
    h, y = t // 4, t % 4
    return w, t, z, x, c, h, y


def wide_at(z, x, c):
    return lax.rem(z + 4, 4) * 4 + x * 2 + c


def tall_at(h, y):
    return h * 4 + lax.rem(y + 4, 4)


def neighbours():
    w, t, z, x, c, h, y = place()
    return {
        "up": (wide_at(z + 1, x, c), t),
        "down": (wide_at(z - 1, x, c), t),
        "side": (wide_at(z, 1 - x, c), t),
        "core": (wide_at(z, x, 1 - c), t),
        "far": (w, tall_at(1 - h, y)),
        "north": (w, tall_at(h, y + 1)),
        "south": (w, tall_at(h, y - 1)),
    }


def greet(partners):
    barrier = pltpu.get_barrier_semaphore()
    for partner in partners:
        pl.semaphore_signal(barrier, inc=1, device_id=partner, device_id_type=MESH)
    pl.semaphore_wait(barrier, len(partners))


def send(src, dst, send_sem, recv_sem, partner):
    copy = pltpu.make_async_remote_copy(
        src_ref=src, dst_ref=dst, send_sem=send_sem, recv_sem=recv_sem,
        device_id=partner, device_id_type=MESH,
    )
    copy.start()
    return copy


def arrived(ref, sem):
    pltpu.make_async_copy(ref, ref, sem).wait()


CHUNKS = 4


def lead_kernel(strip_ref, lead_ref, send_sem, recv_sem, core_sem, local_sem):
    w, t, z, x, c, h, y = place()
    side = neighbours()
    greet(list(side.values()))
    half = B // 2
    rows = half // CHUNKS
    sent = []

    def piece(block, core, n):
        return lead_ref.at[block, pl.ds(core * half + n * rows, rows), :]

    def push(block, core, n, to, sem, slot):
        copy = pltpu.make_async_remote_copy(
            src_ref=piece(block, core, n), dst_ref=piece(block, core, n),
            send_sem=send_sem.at[slot, n], recv_sem=sem.at[block, n],
            device_id=side[to], device_id_type=MESH,
        )
        return copy

    def go(pred, copy):
        if pred is None:
            copy.start()
            sent.append((None, copy))
        else:
            @pl.when(pred)
            def _():
                copy.start()
            sent.append((pred, copy))

    other = 1 - c
    far = tall_at(1 - h, y)
    is_root = w == 0
    own = pltpu.make_async_copy(strip_ref, lead_ref.at[t], local_sem)

    @pl.when(is_root)
    def _():
        own.start()
        own.wait()

    for n in range(CHUNKS):
        go(is_root, push(t, 1, n, "core", recv_sem, 0))
    for n in range(CHUNKS):
        @pl.when(w != 0)
        def _():
            arrived(piece(t, c, n), recv_sem.at[t, n])
        base = x == 0
        go(base & (z == 0), push(t, c, n, "up", recv_sem, 1))
        go(base & (z == 0), push(t, c, n, "down", recv_sem, 2))
        if n % 2 == 0:
            go(base & (z == 1), push(t, c, n, "up", recv_sem, 1))
        else:
            go(base & (z == 3), push(t, c, n, "down", recv_sem, 2))
        go(base, push(t, c, n, "side", recv_sem, 3))
        go(None, push(t, c, n, "far", recv_sem, 4))
        go(None, push(t, c, n, "north", recv_sem, 5))
        go(None, push(t, c, n, "south", recv_sem, 6))
        go(w > 1, push(t, c, n, "core", core_sem, 0))
        go(w == 0, push(t, c, n, "core", core_sem, 7))
    for n in range(CHUNKS):
        arrived(piece(far, c, n), recv_sem.at[far, n])
        go(None, push(far, c, n, "north", recv_sem, 8))
        go(None, push(far, c, n, "south", recv_sem, 9))
        go(None, push(far, c, n, "core", core_sem, 10))
    for n in range(CHUNKS):
        slot = 11
        for hh in (h, 1 - h):
            for step, to in ((-1, "north"), (1, "south")):
                block = tall_at(hh, y + step)
                arrived(piece(block, c, n), recv_sem.at[block, n])
                if n % 2 == (0 if to == "north" else 1):
                    go(None, push(block, c, n, to, recv_sem, slot))
                go(None, push(block, c, n, "core", core_sem, slot + 1))
                slot += 2
    for n in range(CHUNKS):
        for i, hh in enumerate((h, 1 - h)):
            block = tall_at(hh, y + 2)
            arrived(piece(block, c, n), recv_sem.at[block, n])
            go(None, push(block, c, n, "core", core_sem, 19 + i))
    for n in range(CHUNKS):
        for block in range(8):
            @pl.when((w != 0) | (block != t))
            def _():
                arrived(piece(block, other, n), core_sem.at[block, n])
    for pred, copy in sent:
        if pred is None:
            copy.wait_send()
        else:
            @pl.when(pred)
            def _():
                copy.wait_send()


def share_lead(strip):
    return pl.pallas_call(
        lead_kernel,
        out_shape=jax.ShapeDtypeStruct((LEAD // B, B, LEAD), F32),
        in_specs=[vmem_spec()],
        out_specs=vmem_spec(),
        scratch_shapes=[
            pltpu.SemaphoreType.DMA((21, CHUNKS)),
            pltpu.SemaphoreType.DMA((8, CHUNKS)),
            pltpu.SemaphoreType.DMA((8, CHUNKS)),
            pltpu.SemaphoreType.DMA,
        ],
        compiler_params=params(collective_id=0, has_side_effects=True),
        name="share_lead",
    )(strip)


def lane(x, c):
    return jnp.broadcast_to(x[:, c : c + 1], (x.shape[0], B))


def row(x, r):
    return jnp.broadcast_to(x[r : r + 1, :], (8, x.shape[1]))


def factor_block(dref, vref):
    for m in range(B // 8):
        c0 = 8 * m
        p = dref[c0 : c0 + 8, :]
        wp = vref[c0 : c0 + 8, :]
        q = [lane(p, c0 + k) for k in range(8)]
        s = [[row(q[j], i) if j <= i else None for j in range(8)] for i in range(8)]
        f = [[None] * 8 for _ in range(8)]
        dinv = [None] * 8
        for j in range(8):
            dinv[j] = 1.0 / s[j][j]
            for i in range(j + 1, 8):
                f[i][j] = s[i][j] * dinv[j]
            for i in range(j + 1, 8):
                for k in range(j + 1, i + 1):
                    s[i][k] = s[i][k] - f[i][j] * s[k][j]
        r = [row(p, j) for j in range(8)]
        rw = [row(wp, j) for j in range(8)]
        for j in range(8):
            for i in range(j + 1, 8):
                r[i] = r[i] - f[i][j] * r[j]
                rw[i] = rw[i] - f[i][j] * rw[j]
        u = [r[j] * dinv[j] for j in range(8)]
        uw = [rw[j] * dinv[j] for j in range(8)]
        for j in range(7, 0, -1):
            for i in range(j):
                u[i] = u[i] - f[j][i] * u[j]
                uw[i] = uw[i] - f[j][i] * uw[j]
        for v in range(m + 1, B // 8):
            rows = dref[8 * v : 8 * v + 8, :]
            wrows = vref[8 * v : 8 * v + 8, :]
            acc = accw = None
            for j in range(8):
                c = lane(rows, c0 + j)
                acc = c * u[j] if acc is None else acc + c * u[j]
                accw = c * uw[j] if accw is None else accw + c * uw[j]
            dref[8 * v : 8 * v + 8, :] = rows - acc
            vref[8 * v : 8 * v + 8, :] = wrows - accw
        sub = lax.broadcasted_iota(jnp.int32, (8, B), 0)
        out = outw = None
        for j in range(8):
            scale = lax.rsqrt(s[j][j])
            a, b = r[j] * scale, rw[j] * scale
            out = a if out is None else jnp.where(sub == j, a, out)
            outw = b if outw is None else jnp.where(sub == j, b, outw)
        dref[c0 : c0 + 8, :] = out
        vref[c0 : c0 + 8, :] = outw


def split(x):
    high = x.astype(jnp.bfloat16)
    low = (x - high.astype(F32)).astype(jnp.bfloat16)
    return high, low


def dot3(a, b, dims):
    d = functools.partial(lax.dot_general, dimension_numbers=dims, preferred_element_type=F32)
    return d(a[0], b[0]) + (d(a[0], b[1]) + d(a[1], b[0]))


def dot6(a, b, dims):
    return lax.dot_general(a, b, dims, precision=lax.Precision.HIGHEST, preferred_element_type=F32)


def factor_lead(a, w, dblk, vblk, lcol):
    n = a.shape[0]
    blocks = n // B
    ri = lax.broadcasted_iota(jnp.int32, (B, B), 0)
    ci = lax.broadcasted_iota(jnp.int32, (B, B), 1)
    eye = jnp.where(ri == ci, 1.0, 0.0).astype(F32)
    wi = lax.broadcasted_iota(jnp.int32, (B, n), 0)
    wj = lax.broadcasted_iota(jnp.int32, (B, n), 1)
    for i in range(blocks):
        w[i * B : (i + 1) * B, :] = jnp.where(wi + i * B == wj, 1.0, 0.0)

    def step(j, carry):
        o = pl.multiple_of(j * B, B)
        d = a[pl.ds(o, B), pl.ds(o, B)]
        dblk[...] = jnp.where(ri >= ci, d, d.T)
        vblk[...] = eye
        factor_block(dblk, vblk)
        a[pl.ds(o, B), pl.ds(o, B)] = jnp.where(ri <= ci, dblk[...], 0.0).T
        winv = vblk[...]
        wrow = dot6(winv, w[pl.ds(o, B), :], NN)
        w[pl.ds(o, B), :] = wrow

        def solve(i, c):
            r = pl.multiple_of(i * B, B)
            solved = dot6(a[pl.ds(r, B), pl.ds(o, B)], winv, NT)
            a[pl.ds(r, B), pl.ds(o, B)] = solved
            lcol[pl.ds(r, B), :] = solved
            return c

        lax.fori_loop(j + 1, blocks, solve, 0)

        def update(i, c):
            r = pl.multiple_of(i * B, B)
            mine = lcol[pl.ds(r, B), :]
            w[pl.ds(r, B), :] -= dot6(mine, wrow, NN)

            def cols(k, cc):
                s = pl.multiple_of(k * B, B)
                a[pl.ds(r, B), pl.ds(s, B)] -= dot6(mine, lcol[pl.ds(s, B), :], NT)
                return cc

            lax.fori_loop(j + 1, i + 1, cols, 0)
            return c

        lax.fori_loop(j + 1, blocks, update, 0)
        return carry

    lax.fori_loop(0, blocks, step, 0)


def factor_kernel(lead_ref, strip_ref, solved_ref, shown_ref, a, w, dblk, vblk, lcol):
    wide = lax.axis_index("wide")
    tall = lax.axis_index("tall")
    a[...] = lead_ref[...]
    factor_lead(a, w, dblk, vblk, lcol)
    shown_ref[...] = a[pl.ds(pl.multiple_of(tall * B, B), B), :]
    solved = dot6(strip_ref[...], w[...], NT)
    cols = lax.broadcasted_iota(jnp.int32, solved.shape, 1)
    keep = (wide > 0) | ((tall >= PANEL // B) & (cols < PANEL))
    solved_ref[...] = jnp.where(keep, solved, 0.0)


def factor_and_solve(lead, strip):
    return pl.pallas_call(
        factor_kernel,
        out_shape=(jax.ShapeDtypeStruct((B, LEAD), F32),) * 2,
        in_specs=[vmem_spec()] * 2,
        out_specs=(vmem_spec(),) * 2,
        scratch_shapes=[
            pltpu.VMEM((LEAD, LEAD), F32),
            pltpu.VMEM((LEAD, LEAD), F32),
            pltpu.VMEM((B, B), F32),
            pltpu.VMEM((B, B), F32),
            pltpu.VMEM((LEAD, B), F32),
        ],
        compiler_params=params(),
        name="factor",
    )(lead, strip)


def share_kernel(mine_ref, rows_ref, cols_ref, hold, send_sem, row_sem, col_sem, local_sem):
    w, t, z, x, c, h, y = place()
    side = neighbours()
    half = B // 2
    target = 2 * lax.rem(w, 8) + h
    quarter = w // 8
    partners = list(side.values())
    greet(partners)
    sent = []
    count = [0]

    def push(ref, sem, to):
        slot = count[0]
        count[0] += 1
        return pltpu.make_async_remote_copy(
            src_ref=ref, dst_ref=ref, send_sem=send_sem.at[slot], recv_sem=sem,
            device_id=side[to], device_id_type=MESH,
        )

    def go(copy, pred=None):
        if pred is None:
            copy.start()
        else:
            @pl.when(pred)
            def _():
                copy.start()
        sent.append((pred, copy))

    def rpiece(k, n):
        return rows_ref.at[k, pl.ds(n * half, half), :]

    def cpiece(q, i, n):
        return cols_ref.at[q * 4 + i, pl.ds(n * half, half), :]

    own = pltpu.make_async_copy(mine_ref, rows_ref.at[w], local_sem.at[0])
    own.start()

    def first(n, to):
        slot = count[0]
        count[0] += 1
        return pltpu.make_async_remote_copy(
            src_ref=mine_ref.at[pl.ds(n * half, half), :], dst_ref=rpiece(w, n),
            send_sem=send_sem.at[slot], recv_sem=row_sem.at[w, n],
            device_id=side[to], device_id_type=MESH,
        )

    for n in range(2):
        for to in ("side", "up", "down", "core"):
            go(first(n, to))
    beside = wide_at(z, 1 - x, c)
    for n in range(2):
        arrived(rpiece(beside, n), row_sem.at[beside, n])
        for to in ("up", "down", "core"):
            go(push(rpiece(beside, n), row_sem.at[beside, n], to))
    for xx in (x, 1 - x):
        for n in range(2):
            for dz, to, part in ((-1, "up", 0), (1, "down", 1)):
                k = wide_at(z + dz, xx, c)
                arrived(rpiece(k, n), row_sem.at[k, n])
                if n == part:
                    go(push(rpiece(k, n), row_sem.at[k, n], to))
                go(push(rpiece(k, n), row_sem.at[k, n], "core"))
    for xx in (x, 1 - x):
        for n in range(2):
            k = wide_at(z + 2, xx, c)
            arrived(rpiece(k, n), row_sem.at[k, n])
            go(push(rpiece(k, n), row_sem.at[k, n], "core"))
    for zz in (z, z - 1, z + 1, z + 2):
        for xx in (x, 1 - x):
            k = wide_at(zz, xx, 1 - c)
            for n in range(2):
                arrived(rpiece(k, n), row_sem.at[k, n])
    own.wait()
    pair = w // 2
    holder = h == c
    for q in range(2):
        k = q * 8 + pair

        @pl.when(holder)
        def _():
            take = pltpu.make_async_copy(rows_ref.at[k], hold.at[q], local_sem.at[1])
            take.start()
            take.wait()
            put = pltpu.make_async_copy(hold.at[q], cols_ref.at[q * 4 + y], local_sem.at[1])
            put.start()
            put.wait()
    for q in range(2):
        for n in range(2):
            @pl.when(jnp.logical_not(holder))
            def _():
                arrived(cpiece(q, y, n), col_sem.at[q, y, n])
            go(push(cpiece(q, y, n), col_sem.at[q, y, n], "far"), holder)
            go(push(cpiece(q, y, n), col_sem.at[q, y, n], "north"))
            go(push(cpiece(q, y, n), col_sem.at[q, y, n], "south"))
    for q in range(2):
        for n in range(2):
            for dy, to, part in ((-1, "north", 0), (1, "south", 1)):
                i = lax.rem(y + dy + 4, 4)
                arrived(cpiece(q, i, n), col_sem.at[q, i, n])
                if n == part:
                    go(push(cpiece(q, i, n), col_sem.at[q, i, n], to))
    for q in range(2):
        for n in range(2):
            i = lax.rem(y + 2, 4)
            arrived(cpiece(q, i, n), col_sem.at[q, i, n])
    for pred, copy in sent:
        if pred is None:
            copy.wait_send()
        else:
            @pl.when(pred)
            def _():
                copy.wait_send()


def share_solved(mine):
    return pl.pallas_call(
        share_kernel,
        out_shape=(
            jax.ShapeDtypeStruct((16, B, LEAD), F32),
            jax.ShapeDtypeStruct((8, B, LEAD), F32),
        ),
        in_specs=[vmem_spec()],
        out_specs=(any_spec(), any_spec()),
        scratch_shapes=[
            pltpu.VMEM((2, B, LEAD), F32),
            pltpu.SemaphoreType.DMA((64,)),
            pltpu.SemaphoreType.DMA((16, 2)),
            pltpu.SemaphoreType.DMA((2, 4, 2)),
            pltpu.SemaphoreType.DMA((2,)),
        ],
        compiler_params=params(collective_id=1, has_side_effects=True),
        name="share_solved",
    )(mine)


def update_kernel(front_ref, rows_ref, cols_ref, shown_ref, out_ref, high, low):
    step = pl.program_id(0)
    wide = lax.axis_index("wide")
    tall = lax.axis_index("tall")

    @pl.when(step == 0)
    def _():
        for i in range(LEAD // B):
            h, l = split(cols_ref[i * B : (i + 1) * B, :])
            high[i * B : (i + 1) * B, :] = h
            low[i * B : (i + 1) * B, :] = l

    mine = rows_ref[...]
    change = dot3(split(mine), (high[...], low[...]), NT)
    out = front_ref[...] - change
    out_ref[...] = out
    for p in range(2):
        @pl.when(wide == p)
        def _():
            out_ref[:, 0:PANEL] = mine[:, p * PANEL : (p + 1) * PANEL]

            @pl.when(step == 0)
            def _():
                r = lax.broadcasted_iota(jnp.int32, (B, PANEL), 0) + tall * B
                c = lax.broadcasted_iota(jnp.int32, (B, PANEL), 1) + p * PANEL
                out_ref[0:B, 0:PANEL] = jnp.where(
                    r >= c, shown_ref[:, p * PANEL : (p + 1) * PANEL], out[0:B, 0:PANEL]
                )


def update(front, rows, cols, shown):
    total, width = front.shape
    chunk = 256
    return pl.pallas_call(
        update_kernel,
        grid=(total // chunk,),
        out_shape=jax.ShapeDtypeStruct(front.shape, F32),
        in_specs=[
            pl.BlockSpec((chunk, width), lambda i: (i, 0)),
            pl.BlockSpec((chunk, LEAD), lambda i: (i, 0)),
            pl.BlockSpec((width, LEAD), lambda i: (0, 0)),
            pl.BlockSpec((B, LEAD), lambda i: (0, 0)),
        ],
        out_specs=pl.BlockSpec((chunk, width), lambda i: (i, 0)),
        scratch_shapes=[pltpu.VMEM((width, LEAD), jnp.bfloat16)] * 2,
        compiler_params=params(),
        name="update",
    )(front, rows, cols, shown)


def body(initial, child_tiles, child_targets):
    wides = lax.axis_size("wide")
    cols = lax.all_to_all(child_targets[:, 1], "tall", split_axis=0, concat_axis=0, tiled=True)
    tiles = lax.all_to_all(child_tiles, "tall", split_axis=0, concat_axis=0, tiled=True)
    slab, strip = add_tiles(initial, tiles, cols, wides)
    lead = share_lead(strip)
    slab, lead = lax.optimization_barrier((slab, lead))
    front = lax.all_to_all(slab, "wide", split_axis=0, concat_axis=0, tiled=True)
    solved, shown = factor_and_solve(lead.reshape(LEAD, LEAD), strip)
    rows, columns = share_solved(solved)
    front = front.reshape(-1, slab.shape[2])
    return update(front, rows.reshape(-1, LEAD), columns.reshape(-1, LEAD), shown)


def solution(mesh):
    return jax.shard_map(
        body,
        mesh=mesh,
        in_specs=(
            P(("wide", "tall"), None),
            P(("wide", "tall"), None, None),
            P(("wide", "tall"), None),
        ),
        out_specs=P("tall", "wide"),
        check_vma=False,
    )
```

```python
import functools

import jax
import jax.numpy as jnp
from jax import lax
from jax.experimental import pallas as pl
from jax.experimental.pallas import tpu as pltpu
from jax.sharding import PartitionSpec as P

PANEL = 512
LEAD = 1024
B = 128
PADDED = LEAD + B
MESH = pl.DeviceIdType.MESH
NT = (((1,), (1,)), ((), ()))
NN = (((1,), (0,)), ((), ()))
VMEM_LIMIT = 60 * 1024 * 1024
F32 = jnp.float32


def vmem_spec():
    return pl.BlockSpec(memory_space=pltpu.VMEM)


def any_spec():
    return pl.BlockSpec(memory_space=pl.ANY)


def params(**more):
    return pltpu.CompilerParams(vmem_limit_bytes=VMEM_LIMIT, **more)


def add_kernel(cols_ref, initial_ref, tiles_ref, out_ref, strip_ref, acc, tiles, sem_in, sem_tile, sem_out, sem_strip):
    wides = acc.shape[0]
    halves = acc.shape[2] // PANEL
    count = tiles.shape[0]
    loads = []
    for q in range(halves):
        for w in range(wides):
            at = (q * wides + w) * PANEL
            loads.append(
                pltpu.make_async_copy(
                    initial_ref.at[:, at : at + PANEL],
                    acc.at[w, :, q * PANEL : (q + 1) * PANEL],
                    sem_in.at[q * wides + w],
                )
            )
    tile_load = pltpu.make_async_copy(tiles_ref, tiles, sem_tile)
    for load in loads:
        load.start()
    tile_load.start()
    for load in loads:
        load.wait()
    tile_load.wait()
    per_panel = PANEL // B

    def add(n, carry):
        col = cols_ref[n]
        block = col // per_panel
        at = pl.multiple_of((block // wides) * PANEL + (col % per_panel) * B, B)
        acc[block % wides, :, pl.ds(at, B)] += tiles[n]
        return carry

    lax.fori_loop(0, count, add, 0)
    stores = [
        pltpu.make_async_copy(acc.at[0, :, 0:PANEL], strip_ref.at[:, 0:PANEL], sem_strip.at[0]),
        pltpu.make_async_copy(acc.at[1, :, 0:PANEL], strip_ref.at[:, PANEL:LEAD], sem_strip.at[1]),
    ]
    for w in range(wides):
        stores.append(pltpu.make_async_copy(acc.at[w], out_ref.at[w], sem_out.at[w]))
    for store in stores:
        store.start()
    for store in stores:
        store.wait()


def add_tiles(initial, tiles, cols, wides):
    rows, order = initial.shape
    count = tiles.shape[0]
    width = order // wides
    return pl.pallas_call(
        add_kernel,
        grid_spec=pltpu.PrefetchScalarGridSpec(
            num_scalar_prefetch=1,
            grid=(1,),
            in_specs=[any_spec(), any_spec()],
            out_specs=[any_spec(), any_spec()],
            scratch_shapes=[
                pltpu.VMEM((wides, rows, width), F32),
                pltpu.VMEM((count, B, B), F32),
                pltpu.SemaphoreType.DMA((order // PANEL,)),
                pltpu.SemaphoreType.DMA,
                pltpu.SemaphoreType.DMA((wides,)),
                pltpu.SemaphoreType.DMA((2,)),
            ],
        ),
        out_shape=[
            jax.ShapeDtypeStruct((wides, rows, width), F32),
            jax.ShapeDtypeStruct((rows, LEAD), F32),
        ],
        compiler_params=params(),
        name="add_tiles",
    )(cols, initial, tiles)


def place():
    w = lax.axis_index("wide")
    t = lax.axis_index("tall")
    z, x, c = w // 4, (w // 2) % 2, w % 2
    h, y = t // 4, t % 4
    return w, t, z, x, c, h, y


def wide_at(z, x, c):
    return lax.rem(z + 4, 4) * 4 + x * 2 + c


def tall_at(h, y):
    return h * 4 + lax.rem(y + 4, 4)


def neighbours():
    w, t, z, x, c, h, y = place()
    return {
        "up": (wide_at(z + 1, x, c), t),
        "down": (wide_at(z - 1, x, c), t),
        "side": (wide_at(z, 1 - x, c), t),
        "core": (wide_at(z, x, 1 - c), t),
        "far": (w, tall_at(1 - h, y)),
        "north": (w, tall_at(h, y + 1)),
        "south": (w, tall_at(h, y - 1)),
    }


def greet(partners):
    barrier = pltpu.get_barrier_semaphore()
    for partner in partners:
        pl.semaphore_signal(barrier, inc=1, device_id=partner, device_id_type=MESH)
    pl.semaphore_wait(barrier, len(partners))


def send(src, dst, send_sem, recv_sem, partner):
    copy = pltpu.make_async_remote_copy(
        src_ref=src, dst_ref=dst, send_sem=send_sem, recv_sem=recv_sem,
        device_id=partner, device_id_type=MESH,
    )
    copy.start()
    return copy


def arrived(ref, sem):
    pltpu.make_async_copy(ref, ref, sem).wait()


CHUNKS = 4


def lead_kernel(strip_ref, lead_ref, send_sem, recv_sem, core_sem, local_sem):
    w, t, z, x, c, h, y = place()
    side = neighbours()
    greet(list(side.values()))
    half = B // 2
    rows = half // CHUNKS
    sent = []

    def piece(block, core, n):
        return lead_ref.at[block, pl.ds(core * half + n * rows, rows), :]

    def push(block, core, n, to, sem, slot):
        copy = pltpu.make_async_remote_copy(
            src_ref=piece(block, core, n), dst_ref=piece(block, core, n),
            send_sem=send_sem.at[slot, n], recv_sem=sem.at[block, n],
            device_id=side[to], device_id_type=MESH,
        )
        return copy

    def go(pred, copy):
        if pred is None:
            copy.start()
            sent.append((None, copy))
        else:
            @pl.when(pred)
            def _():
                copy.start()
            sent.append((pred, copy))

    other = 1 - c
    far = tall_at(1 - h, y)
    is_root = w == 0
    own = pltpu.make_async_copy(strip_ref, lead_ref.at[t], local_sem)

    @pl.when(is_root)
    def _():
        own.start()
        own.wait()

    for n in range(CHUNKS):
        go(is_root, push(t, 1, n, "core", recv_sem, 0))
    for n in range(CHUNKS):
        @pl.when(w != 0)
        def _():
            arrived(piece(t, c, n), recv_sem.at[t, n])
        base = x == 0
        go(base & (z == 0), push(t, c, n, "up", recv_sem, 1))
        go(base & (z == 0), push(t, c, n, "down", recv_sem, 2))
        if n % 2 == 0:
            go(base & (z == 1), push(t, c, n, "up", recv_sem, 1))
        else:
            go(base & (z == 3), push(t, c, n, "down", recv_sem, 2))
        go(base, push(t, c, n, "side", recv_sem, 3))
        go(None, push(t, c, n, "far", recv_sem, 4))
        go(None, push(t, c, n, "north", recv_sem, 5))
        go(None, push(t, c, n, "south", recv_sem, 6))
        go(w > 1, push(t, c, n, "core", core_sem, 0))
        go(w == 0, push(t, c, n, "core", core_sem, 7))
    for n in range(CHUNKS):
        arrived(piece(far, c, n), recv_sem.at[far, n])
        go(None, push(far, c, n, "north", recv_sem, 8))
        go(None, push(far, c, n, "south", recv_sem, 9))
        go(None, push(far, c, n, "core", core_sem, 10))
    for n in range(CHUNKS):
        slot = 11
        for hh in (h, 1 - h):
            for step, to in ((-1, "north"), (1, "south")):
                block = tall_at(hh, y + step)
                arrived(piece(block, c, n), recv_sem.at[block, n])
                if n % 2 == (0 if to == "north" else 1):
                    go(None, push(block, c, n, to, recv_sem, slot))
                go(None, push(block, c, n, "core", core_sem, slot + 1))
                slot += 2
    for n in range(CHUNKS):
        for i, hh in enumerate((h, 1 - h)):
            block = tall_at(hh, y + 2)
            arrived(piece(block, c, n), recv_sem.at[block, n])
            go(None, push(block, c, n, "core", core_sem, 19 + i))
    for n in range(CHUNKS):
        for block in range(8):
            @pl.when((w != 0) | (block != t))
            def _():
                arrived(piece(block, other, n), core_sem.at[block, n])
    for pred, copy in sent:
        if pred is None:
            copy.wait_send()
        else:
            @pl.when(pred)
            def _():
                copy.wait_send()


def share_lead(strip):
    return pl.pallas_call(
        lead_kernel,
        out_shape=jax.ShapeDtypeStruct((LEAD // B, B, LEAD), F32),
        in_specs=[vmem_spec()],
        out_specs=vmem_spec(),
        scratch_shapes=[
            pltpu.SemaphoreType.DMA((21, CHUNKS)),
            pltpu.SemaphoreType.DMA((8, CHUNKS)),
            pltpu.SemaphoreType.DMA((8, CHUNKS)),
            pltpu.SemaphoreType.DMA,
        ],
        compiler_params=params(collective_id=0, has_side_effects=True),
        name="share_lead",
    )(strip)


def lane(x, c):
    return jnp.broadcast_to(x[:, c : c + 1], (x.shape[0], B))


def row(x, r):
    return jnp.broadcast_to(x[r : r + 1, :], (8, x.shape[1]))


def factor_block(dref, vref):
    for m in range(B // 8):
        c0 = 8 * m
        p = dref[c0 : c0 + 8, :]
        wp = vref[c0 : c0 + 8, :]
        q = [lane(p, c0 + k) for k in range(8)]
        s = [[row(q[j], i) if j <= i else None for j in range(8)] for i in range(8)]
        f = [[None] * 8 for _ in range(8)]
        dinv = [None] * 8
        for j in range(8):
            dinv[j] = 1.0 / s[j][j]
            for i in range(j + 1, 8):
                f[i][j] = s[i][j] * dinv[j]
            for i in range(j + 1, 8):
                for k in range(j + 1, i + 1):
                    s[i][k] = s[i][k] - f[i][j] * s[k][j]
        r = [row(p, j) for j in range(8)]
        rw = [row(wp, j) for j in range(8)]
        for j in range(8):
            for i in range(j + 1, 8):
                r[i] = r[i] - f[i][j] * r[j]
                rw[i] = rw[i] - f[i][j] * rw[j]
        u = [r[j] * dinv[j] for j in range(8)]
        uw = [rw[j] * dinv[j] for j in range(8)]
        for j in range(7, 0, -1):
            for i in range(j):
                u[i] = u[i] - f[j][i] * u[j]
                uw[i] = uw[i] - f[j][i] * uw[j]
        for v in range(m + 1, B // 8):
            rows = dref[8 * v : 8 * v + 8, :]
            wrows = vref[8 * v : 8 * v + 8, :]
            acc = accw = None
            for j in range(8):
                c = lane(rows, c0 + j)
                acc = c * u[j] if acc is None else acc + c * u[j]
                accw = c * uw[j] if accw is None else accw + c * uw[j]
            dref[8 * v : 8 * v + 8, :] = rows - acc
            vref[8 * v : 8 * v + 8, :] = wrows - accw
        sub = lax.broadcasted_iota(jnp.int32, (8, B), 0)
        out = outw = None
        for j in range(8):
            scale = lax.rsqrt(s[j][j])
            a, b = r[j] * scale, rw[j] * scale
            out = a if out is None else jnp.where(sub == j, a, out)
            outw = b if outw is None else jnp.where(sub == j, b, outw)
        dref[c0 : c0 + 8, :] = out
        vref[c0 : c0 + 8, :] = outw


def split(x):
    high = x.astype(jnp.bfloat16)
    low = (x - high.astype(F32)).astype(jnp.bfloat16)
    return high, low


def dot3(a, b, dims):
    d = functools.partial(lax.dot_general, dimension_numbers=dims, preferred_element_type=F32)
    return d(a[0], b[0]) + (d(a[0], b[1]) + d(a[1], b[0]))


def dot6(a, b, dims):
    return lax.dot_general(a, b, dims, precision=lax.Precision.HIGHEST, preferred_element_type=F32)


def thirds(x):
    high = x.astype(jnp.bfloat16)
    rest = x - high.astype(F32)
    mid = rest.astype(jnp.bfloat16)
    low = (rest - mid.astype(F32)).astype(jnp.bfloat16)
    return high, mid, low


def left6(x):
    h, m, l = thirds(x)
    return jnp.concatenate([h, m, h, m, h, l], axis=1)


def right6(x, axis):
    h, m, l = thirds(x)
    return jnp.concatenate([h, h, m, m, l, h], axis=axis)


def product(a, b, dims):
    return lax.dot_general(a, b, dims, preferred_element_type=F32)


def factor_lead(a, w, dblk, vblk, lleft, lright):
    n = LEAD
    blocks = n // B
    wide = 2 * B
    ri = lax.broadcasted_iota(jnp.int32, (B, B), 0)
    ci = lax.broadcasted_iota(jnp.int32, (B, B), 1)
    eye = jnp.where(ri == ci, 1.0, 0.0).astype(F32)
    wi = lax.broadcasted_iota(jnp.int32, (B, n), 0)
    wj = lax.broadcasted_iota(jnp.int32, (B, n), 1)
    for i in range(blocks):
        w[i * B : (i + 1) * B, :] = jnp.where(wi + i * B == wj, 1.0, 0.0)
    w[n:, :] = jnp.zeros((B, n), F32)
    a[0:n, n:] = jnp.zeros((n, B), F32)
    a[n:, :] = jnp.zeros((B, n + B), F32)

    def step(j, carry):
        o = pl.multiple_of(j * B, B)
        d = a[pl.ds(o, B), pl.ds(o, B)]
        dblk[...] = jnp.where(ri >= ci, d, d.T)
        vblk[...] = eye
        factor_block(dblk, vblk)
        a[pl.ds(o, B), pl.ds(o, B)] = jnp.where(ri <= ci, dblk[...], 0.0).T
        winv = vblk[...]
        wright = right6(winv, 1)
        wleft = left6(winv)
        pairs = (blocks - j) // 2

        def below(m):
            return pl.multiple_of(o + B + m * wide, B)

        def solve(m, c):
            r = below(m)
            solved = product(left6(a[pl.ds(r, wide), pl.ds(o, B)]), wright, NT)
            a[pl.ds(r, wide), pl.ds(o, B)] = solved
            lleft[pl.ds(r, wide), :] = left6(solved)
            lright[pl.ds(r, wide), :] = right6(solved, 1)
            return c

        lax.fori_loop(0, pairs, solve, 0)

        def reduce(k, c):
            at = pl.multiple_of(k * wide, wide)
            wrow = product(wleft, right6(w[pl.ds(o, B), pl.ds(at, wide)], 0), NN)
            w[pl.ds(o, B), pl.ds(at, wide)] = wrow
            right = right6(wrow, 0)

            def down(m, cc):
                r = below(m)
                w[pl.ds(r, wide), pl.ds(at, wide)] -= product(lleft[pl.ds(r, wide), :], right, NN)
                return cc

            lax.fori_loop(0, pairs, down, 0)
            return c

        lax.fori_loop(0, j // 2 + 1, reduce, 0)

        def update(k, c):
            s = below(k)
            right = lright[pl.ds(s, wide), :]

            def down(m, cc):
                r = below(m)
                a[pl.ds(r, wide), pl.ds(s, wide)] -= product(lleft[pl.ds(r, wide), :], right, NT)
                return cc

            lax.fori_loop(k, pairs, down, 0)
            return c

        lax.fori_loop(0, pairs, update, 0)
        return carry

    lax.fori_loop(0, blocks, step, 0)


def factor_kernel(lead_ref, strip_ref, solved_ref, shown_ref, a, w, dblk, vblk, lleft, lright):
    wide = lax.axis_index("wide")
    tall = lax.axis_index("tall")
    a[0:LEAD, 0:LEAD] = lead_ref[...]
    factor_lead(a, w, dblk, vblk, lleft, lright)
    shown_ref[...] = a[pl.ds(pl.multiple_of(tall * B, B), B), 0:LEAD]
    solved = dot6(strip_ref[...], w[0:LEAD, :], NT)
    cols = lax.broadcasted_iota(jnp.int32, solved.shape, 1)
    keep = (wide > 0) | ((tall >= PANEL // B) & (cols < PANEL))
    solved_ref[...] = jnp.where(keep, solved, 0.0)


def factor_and_solve(lead, strip):
    return pl.pallas_call(
        factor_kernel,
        out_shape=(jax.ShapeDtypeStruct((B, LEAD), F32),) * 2,
        in_specs=[vmem_spec()] * 2,
        out_specs=(vmem_spec(),) * 2,
        scratch_shapes=[
            pltpu.VMEM((PADDED, PADDED), F32),
            pltpu.VMEM((PADDED, LEAD), F32),
            pltpu.VMEM((B, B), F32),
            pltpu.VMEM((B, B), F32),
            pltpu.VMEM((PADDED, 6 * B), jnp.bfloat16),
            pltpu.VMEM((PADDED, 6 * B), jnp.bfloat16),
        ],
        compiler_params=params(),
        name="factor",
    )(lead, strip)


def share_kernel(mine_ref, rows_ref, cols_ref, send_sem, row_sem, col_sem, local_sem):
    w, t, z, x, c, h, y = place()
    side = neighbours()
    half = B // 2
    target = 2 * lax.rem(w, 8) + h
    quarter = w // 8
    pair = w // 2
    holder = h == c
    away = target != w
    barrier = pltpu.get_barrier_semaphore()
    extra = [(away, target)] + [(holder & (q * 8 + pair != w), q * 8 + pair) for q in range(2)]
    for partner in side.values():
        pl.semaphore_signal(barrier, inc=1, device_id=partner, device_id_type=MESH)
    for pred, k in extra:
        @pl.when(pred)
        def _():
            pl.semaphore_signal(barrier, inc=1, device_id=(k, t), device_id_type=MESH)
    peers = len(side)
    for pred, _ in extra:
        peers = peers + jnp.where(pred, 1, 0)
    pl.semaphore_wait(barrier, peers)
    sent = []
    count = [0]

    def copy_to(src, dst, sem, device):
        slot = count[0]
        count[0] += 1
        return pltpu.make_async_remote_copy(
            src_ref=src, dst_ref=dst, send_sem=send_sem.at[slot], recv_sem=sem,
            device_id=device, device_id_type=MESH,
        )

    def push(ref, sem, to):
        return copy_to(ref, ref, sem, side[to])

    def go(copy, pred=None):
        if pred is None:
            copy.start()
        else:
            @pl.when(pred)
            def _():
                copy.start()
        sent.append((pred, copy))

    def rpiece(k, n):
        return rows_ref.at[k, pl.ds(n * half, half), :]

    def cpiece(q, i, n):
        return cols_ref.at[q * 4 + i, pl.ds(n * half, half), :]

    def mpiece(n):
        return mine_ref.at[pl.ds(n * half, half), :]

    own = pltpu.make_async_copy(mine_ref, rows_ref.at[w], local_sem.at[0])
    own.start()
    kept = pltpu.make_async_copy(mine_ref, cols_ref.at[quarter * 4 + y], local_sem.at[1])

    @pl.when(jnp.logical_not(away))
    def _():
        kept.start()

    for n in range(2):
        go(copy_to(mpiece(n), cpiece(quarter, y, n), col_sem.at[quarter, y, n], (target, t)), away)
        for to in ("side", "up", "down", "core"):
            go(copy_to(mpiece(n), rpiece(w, n), row_sem.at[w, n], side[to]))

    @pl.when(jnp.logical_not(away))
    def _():
        kept.wait()

    beside = wide_at(z, 1 - x, c)
    for n in range(2):
        arrived(rpiece(beside, n), row_sem.at[beside, n])
        for to in ("up", "down", "core"):
            go(push(rpiece(beside, n), row_sem.at[beside, n], to))

    def take(q, n):
        @pl.when(jnp.logical_not(holder) | (q * 8 + pair != w))
        def _():
            arrived(cpiece(q, y, n), col_sem.at[q, y, n])

        go(push(cpiece(q, y, n), col_sem.at[q, y, n], "far"), holder)
        go(push(cpiece(q, y, n), col_sem.at[q, y, n], "north"))
        go(push(cpiece(q, y, n), col_sem.at[q, y, n], "south"))

    def next_rows(xx, n):
        for dz, to, part in ((-1, "up", 0), (1, "down", 1)):
            k = wide_at(z + dz, xx, c)
            arrived(rpiece(k, n), row_sem.at[k, n])
            if n == part:
                go(push(rpiece(k, n), row_sem.at[k, n], to))
            go(push(rpiece(k, n), row_sem.at[k, n], "core"))

    for q in range(2):
        take(q, 0)
    for n in range(2):
        next_rows(x, n)
    for q in range(2):
        take(q, 1)
    for n in range(2):
        next_rows(1 - x, n)
    for q in range(2):
        for n in range(2):
            for dy, to, part in ((-1, "north", 0), (1, "south", 1)):
                i = lax.rem(y + dy + 4, 4)
                arrived(cpiece(q, i, n), col_sem.at[q, i, n])
                if n == part:
                    go(push(cpiece(q, i, n), col_sem.at[q, i, n], to))
    for xx in (x, 1 - x):
        for n in range(2):
            k = wide_at(z + 2, xx, c)
            arrived(rpiece(k, n), row_sem.at[k, n])
            go(push(rpiece(k, n), row_sem.at[k, n], "core"))
    for q in range(2):
        for n in range(2):
            i = lax.rem(y + 2, 4)
            arrived(cpiece(q, i, n), col_sem.at[q, i, n])
    for zz in (z, z - 1, z + 1, z + 2):
        for xx in (x, 1 - x):
            k = wide_at(zz, xx, 1 - c)
            for n in range(2):
                arrived(rpiece(k, n), row_sem.at[k, n])
    own.wait()
    for pred, copy in sent:
        if pred is None:
            copy.wait_send()
        else:
            @pl.when(pred)
            def _():
                copy.wait_send()


def share_solved(mine):
    return pl.pallas_call(
        share_kernel,
        out_shape=(
            jax.ShapeDtypeStruct((16, B, LEAD), F32),
            jax.ShapeDtypeStruct((8, B, LEAD), F32),
        ),
        in_specs=[vmem_spec()],
        out_specs=(any_spec(), any_spec()),
        scratch_shapes=[
            pltpu.SemaphoreType.DMA((64,)),
            pltpu.SemaphoreType.DMA((16, 2)),
            pltpu.SemaphoreType.DMA((2, 4, 2)),
            pltpu.SemaphoreType.DMA((2,)),
        ],
        compiler_params=params(collective_id=1, has_side_effects=True),
        name="share_solved",
    )(mine)


def update_kernel(front_ref, rows_ref, cols_ref, shown_ref, out_ref, high, low):
    step = pl.program_id(0)
    wide = lax.axis_index("wide")
    tall = lax.axis_index("tall")

    @pl.when(step == 0)
    def _():
        for i in range(LEAD // B):
            h, l = split(cols_ref[i * B : (i + 1) * B, :])
            high[i * B : (i + 1) * B, :] = h
            low[i * B : (i + 1) * B, :] = l

    mine = rows_ref[...]
    change = dot3(split(mine), (high[...], low[...]), NT)
    out = front_ref[...] - change
    out_ref[...] = out
    for p in range(2):
        @pl.when(wide == p)
        def _():
            out_ref[:, 0:PANEL] = mine[:, p * PANEL : (p + 1) * PANEL]

            @pl.when(step == 0)
            def _():
                r = lax.broadcasted_iota(jnp.int32, (B, PANEL), 0) + tall * B
                c = lax.broadcasted_iota(jnp.int32, (B, PANEL), 1) + p * PANEL
                out_ref[0:B, 0:PANEL] = jnp.where(
                    r >= c, shown_ref[:, p * PANEL : (p + 1) * PANEL], out[0:B, 0:PANEL]
                )


def update(front, rows, cols, shown):
    total, width = front.shape
    chunk = 256
    return pl.pallas_call(
        update_kernel,
        grid=(total // chunk,),
        out_shape=jax.ShapeDtypeStruct(front.shape, F32),
        in_specs=[
            pl.BlockSpec((chunk, width), lambda i: (i, 0)),
            pl.BlockSpec((chunk, LEAD), lambda i: (i, 0)),
            pl.BlockSpec((width, LEAD), lambda i: (0, 0)),
            pl.BlockSpec((B, LEAD), lambda i: (0, 0)),
        ],
        out_specs=pl.BlockSpec((chunk, width), lambda i: (i, 0)),
        scratch_shapes=[pltpu.VMEM((width, LEAD), jnp.bfloat16)] * 2,
        compiler_params=params(),
        name="update",
    )(front, rows, cols, shown)


def body(initial, child_tiles, child_targets):
    wides = lax.axis_size("wide")
    cols = lax.all_to_all(child_targets[:, 1], "tall", split_axis=0, concat_axis=0, tiled=True)
    tiles = lax.all_to_all(child_tiles, "tall", split_axis=0, concat_axis=0, tiled=True)
    slab, strip = add_tiles(initial, tiles, cols, wides)
    lead = share_lead(strip)
    slab, lead = lax.optimization_barrier((slab, lead))
    front = lax.all_to_all(slab, "wide", split_axis=0, concat_axis=0, tiled=True)
    solved, shown = factor_and_solve(lead.reshape(LEAD, LEAD), strip)
    rows, columns = share_solved(solved)
    front = front.reshape(-1, slab.shape[2])
    return update(front, rows.reshape(-1, LEAD), columns.reshape(-1, LEAD), shown)


def solution(mesh):
    return jax.shard_map(
        body,
        mesh=mesh,
        in_specs=(
            P(("wide", "tall"), None),
            P(("wide", "tall"), None, None),
            P(("wide", "tall"), None),
        ),
        out_specs=P("tall", "wide"),
        check_vma=False,
    )
```

```python
import functools

import jax
import jax.numpy as jnp
from jax import lax
from jax.experimental import pallas as pl
from jax.experimental.pallas import tpu as pltpu
from jax.sharding import PartitionSpec as P

PANEL = 512
LEAD = 1024
B = 128
PADDED = LEAD + B
MESH = pl.DeviceIdType.MESH
NT = (((1,), (1,)), ((), ()))
NN = (((1,), (0,)), ((), ()))
VMEM_LIMIT = 60 * 1024 * 1024
F32 = jnp.float32


def vmem_spec():
    return pl.BlockSpec(memory_space=pltpu.VMEM)


def any_spec():
    return pl.BlockSpec(memory_space=pl.ANY)


def params(**more):
    return pltpu.CompilerParams(vmem_limit_bytes=VMEM_LIMIT, **more)


def add_kernel(cols_ref, initial_ref, tiles_ref, out_ref, strip_ref, acc, tiles, sem_in, sem_tile, sem_out, sem_strip):
    wides = acc.shape[0]
    halves = acc.shape[2] // PANEL
    count = tiles.shape[0]
    loads = []
    for q in range(halves):
        for w in range(wides):
            at = (q * wides + w) * PANEL
            loads.append(
                pltpu.make_async_copy(
                    initial_ref.at[:, at : at + PANEL],
                    acc.at[w, :, q * PANEL : (q + 1) * PANEL],
                    sem_in.at[q * wides + w],
                )
            )
    tile_load = pltpu.make_async_copy(tiles_ref, tiles, sem_tile)
    for load in loads:
        load.start()
    tile_load.start()
    for load in loads:
        load.wait()
    tile_load.wait()
    per_panel = PANEL // B

    def add(n, carry):
        col = cols_ref[n]
        block = col // per_panel
        at = pl.multiple_of((block // wides) * PANEL + (col % per_panel) * B, B)
        acc[block % wides, :, pl.ds(at, B)] += tiles[n]
        return carry

    lax.fori_loop(0, count, add, 0)
    stores = [
        pltpu.make_async_copy(acc.at[0, :, 0:PANEL], strip_ref.at[:, 0:PANEL], sem_strip.at[0]),
        pltpu.make_async_copy(acc.at[1, :, 0:PANEL], strip_ref.at[:, PANEL:LEAD], sem_strip.at[1]),
    ]
    for w in range(wides):
        stores.append(pltpu.make_async_copy(acc.at[w], out_ref.at[w], sem_out.at[w]))
    for store in stores:
        store.start()
    for store in stores:
        store.wait()


def add_tiles(initial, tiles, cols, wides):
    rows, order = initial.shape
    count = tiles.shape[0]
    width = order // wides
    return pl.pallas_call(
        add_kernel,
        grid_spec=pltpu.PrefetchScalarGridSpec(
            num_scalar_prefetch=1,
            grid=(1,),
            in_specs=[any_spec(), any_spec()],
            out_specs=[any_spec(), any_spec()],
            scratch_shapes=[
                pltpu.VMEM((wides, rows, width), F32),
                pltpu.VMEM((count, B, B), F32),
                pltpu.SemaphoreType.DMA((order // PANEL,)),
                pltpu.SemaphoreType.DMA,
                pltpu.SemaphoreType.DMA((wides,)),
                pltpu.SemaphoreType.DMA((2,)),
            ],
        ),
        out_shape=[
            jax.ShapeDtypeStruct((wides, rows, width), F32),
            jax.ShapeDtypeStruct((rows, LEAD), F32),
        ],
        compiler_params=params(),
        name="add_tiles",
    )(cols, initial, tiles)


def place():
    w = lax.axis_index("wide")
    t = lax.axis_index("tall")
    z, x, c = w // 4, (w // 2) % 2, w % 2
    h, y = t // 4, t % 4
    return w, t, z, x, c, h, y


def wide_at(z, x, c):
    return lax.rem(z + 4, 4) * 4 + x * 2 + c


def tall_at(h, y):
    return h * 4 + lax.rem(y + 4, 4)


def neighbours():
    w, t, z, x, c, h, y = place()
    return {
        "up": (wide_at(z + 1, x, c), t),
        "down": (wide_at(z - 1, x, c), t),
        "side": (wide_at(z, 1 - x, c), t),
        "core": (wide_at(z, x, 1 - c), t),
        "far": (w, tall_at(1 - h, y)),
        "north": (w, tall_at(h, y + 1)),
        "south": (w, tall_at(h, y - 1)),
    }


def greet(partners):
    barrier = pltpu.get_barrier_semaphore()
    for partner in partners:
        pl.semaphore_signal(barrier, inc=1, device_id=partner, device_id_type=MESH)
    pl.semaphore_wait(barrier, len(partners))


def send(src, dst, send_sem, recv_sem, partner):
    copy = pltpu.make_async_remote_copy(
        src_ref=src, dst_ref=dst, send_sem=send_sem, recv_sem=recv_sem,
        device_id=partner, device_id_type=MESH,
    )
    copy.start()
    return copy


def arrived(ref, sem):
    pltpu.make_async_copy(ref, ref, sem).wait()


def cols_kernel(src_ref, out_ref, send_sem, recv_sem, local_sem):
    w, t = lax.axis_index("wide"), lax.axis_index("tall")
    talls = src_ref.shape[0]
    greet([(w, lax.rem(t + d, talls)) for d in range(1, talls)])
    own = pltpu.make_async_copy(src_ref.at[t], out_ref.at[t], local_sem)
    own.start()
    sent = []
    for d in range(1, talls):
        to = lax.rem(t + d, talls)
        sent.append(send(src_ref.at[to], out_ref.at[t], send_sem.at[d], recv_sem.at[t], (w, to)))
    for d in range(1, talls):
        source = lax.rem(t + talls - d, talls)
        arrived(out_ref.at[source], recv_sem.at[source])
    own.wait()
    for copy in sent:
        copy.wait_send()


def share_cols(cols, talls):
    each = cols.shape[0] // talls
    padded = jnp.pad(cols.reshape(talls, 1, each), ((0, 0), (0, 7), (0, B - each)))
    got = pl.pallas_call(
        cols_kernel,
        out_shape=jax.ShapeDtypeStruct(padded.shape, padded.dtype),
        in_specs=[vmem_spec()],
        out_specs=vmem_spec(),
        scratch_shapes=[
            pltpu.SemaphoreType.DMA((talls,)),
            pltpu.SemaphoreType.DMA((talls,)),
            pltpu.SemaphoreType.DMA,
        ],
        compiler_params=params(collective_id=2, has_side_effects=True),
        name="share_cols",
    )(padded)
    return got[:, 0, :each].reshape(-1)


CHUNKS = 4


def lead_kernel(strip_ref, lead_ref, send_sem, recv_sem, core_sem, local_sem):
    w, t, z, x, c, h, y = place()
    side = neighbours()
    greet(list(side.values()))
    half = B // 2
    rows = half // CHUNKS
    sent = []

    def piece(block, core, n):
        return lead_ref.at[block, pl.ds(core * half + n * rows, rows), :]

    def push(block, core, n, to, sem, slot):
        copy = pltpu.make_async_remote_copy(
            src_ref=piece(block, core, n), dst_ref=piece(block, core, n),
            send_sem=send_sem.at[slot, n], recv_sem=sem.at[block, n],
            device_id=side[to], device_id_type=MESH,
        )
        return copy

    def go(pred, copy):
        if pred is None:
            copy.start()
            sent.append((None, copy))
        else:
            @pl.when(pred)
            def _():
                copy.start()
            sent.append((pred, copy))

    other = 1 - c
    far = tall_at(1 - h, y)
    is_root = w == 0
    own = pltpu.make_async_copy(strip_ref, lead_ref.at[t], local_sem)

    @pl.when(is_root)
    def _():
        own.start()
        own.wait()

    for n in range(CHUNKS):
        go(is_root, push(t, 1, n, "core", recv_sem, 0))
    for n in range(CHUNKS):
        @pl.when(w != 0)
        def _():
            arrived(piece(t, c, n), recv_sem.at[t, n])
        base = x == 0
        go(base & (z == 0), push(t, c, n, "up", recv_sem, 1))
        go(base & (z == 0), push(t, c, n, "down", recv_sem, 2))
        if n % 2 == 0:
            go(base & (z == 1), push(t, c, n, "up", recv_sem, 1))
        else:
            go(base & (z == 3), push(t, c, n, "down", recv_sem, 2))
        go(base, push(t, c, n, "side", recv_sem, 3))
        go(None, push(t, c, n, "far", recv_sem, 4))
        go(None, push(t, c, n, "north", recv_sem, 5))
        go(None, push(t, c, n, "south", recv_sem, 6))
        go(w > 1, push(t, c, n, "core", core_sem, 0))
        go(w == 0, push(t, c, n, "core", core_sem, 7))
    for n in range(CHUNKS):
        arrived(piece(far, c, n), recv_sem.at[far, n])
        go(None, push(far, c, n, "north", recv_sem, 8))
        go(None, push(far, c, n, "south", recv_sem, 9))
        go(None, push(far, c, n, "core", core_sem, 10))
    for n in range(CHUNKS):
        slot = 11
        for hh in (h, 1 - h):
            for step, to in ((-1, "north"), (1, "south")):
                block = tall_at(hh, y + step)
                arrived(piece(block, c, n), recv_sem.at[block, n])
                if n % 2 == (0 if to == "north" else 1):
                    go(None, push(block, c, n, to, recv_sem, slot))
                go(None, push(block, c, n, "core", core_sem, slot + 1))
                slot += 2
    for n in range(CHUNKS):
        for i, hh in enumerate((h, 1 - h)):
            block = tall_at(hh, y + 2)
            arrived(piece(block, c, n), recv_sem.at[block, n])
            go(None, push(block, c, n, "core", core_sem, 19 + i))
    for n in range(CHUNKS):
        for block in range(8):
            @pl.when((w != 0) | (block != t))
            def _():
                arrived(piece(block, other, n), core_sem.at[block, n])
    for pred, copy in sent:
        if pred is None:
            copy.wait_send()
        else:
            @pl.when(pred)
            def _():
                copy.wait_send()


def share_lead(strip):
    return pl.pallas_call(
        lead_kernel,
        out_shape=jax.ShapeDtypeStruct((LEAD // B, B, LEAD), F32),
        in_specs=[vmem_spec()],
        out_specs=vmem_spec(),
        scratch_shapes=[
            pltpu.SemaphoreType.DMA((21, CHUNKS)),
            pltpu.SemaphoreType.DMA((8, CHUNKS)),
            pltpu.SemaphoreType.DMA((8, CHUNKS)),
            pltpu.SemaphoreType.DMA,
        ],
        compiler_params=params(collective_id=0, has_side_effects=True),
        name="share_lead",
    )(strip)


def lane(x, c):
    return jnp.broadcast_to(x[:, c : c + 1], (x.shape[0], B))


def row(x, r):
    return jnp.broadcast_to(x[r : r + 1, :], (8, x.shape[1]))


def factor_block(dref, vref):
    for m in range(B // 8):
        c0 = 8 * m
        p = dref[c0 : c0 + 8, :]
        wp = vref[c0 : c0 + 8, :]
        q = [lane(p, c0 + k) for k in range(8)]
        s = [[row(q[j], i) if j <= i else None for j in range(8)] for i in range(8)]
        f = [[None] * 8 for _ in range(8)]
        dinv = [None] * 8
        for j in range(8):
            dinv[j] = 1.0 / s[j][j]
            for i in range(j + 1, 8):
                f[i][j] = s[i][j] * dinv[j]
            for i in range(j + 1, 8):
                for k in range(j + 1, i + 1):
                    s[i][k] = s[i][k] - f[i][j] * s[k][j]
        r = [row(p, j) for j in range(8)]
        rw = [row(wp, j) for j in range(8)]
        for j in range(8):
            for i in range(j + 1, 8):
                r[i] = r[i] - f[i][j] * r[j]
                rw[i] = rw[i] - f[i][j] * rw[j]
        u = [r[j] * dinv[j] for j in range(8)]
        uw = [rw[j] * dinv[j] for j in range(8)]
        for j in range(7, 0, -1):
            for i in range(j):
                u[i] = u[i] - f[j][i] * u[j]
                uw[i] = uw[i] - f[j][i] * uw[j]
        for v in range(m + 1, B // 8):
            rows = dref[8 * v : 8 * v + 8, :]
            wrows = vref[8 * v : 8 * v + 8, :]
            acc = accw = None
            for j in range(8):
                c = lane(rows, c0 + j)
                acc = c * u[j] if acc is None else acc + c * u[j]
                accw = c * uw[j] if accw is None else accw + c * uw[j]
            dref[8 * v : 8 * v + 8, :] = rows - acc
            vref[8 * v : 8 * v + 8, :] = wrows - accw
        sub = lax.broadcasted_iota(jnp.int32, (8, B), 0)
        out = outw = None
        for j in range(8):
            scale = lax.rsqrt(s[j][j])
            a, b = r[j] * scale, rw[j] * scale
            out = a if out is None else jnp.where(sub == j, a, out)
            outw = b if outw is None else jnp.where(sub == j, b, outw)
        dref[c0 : c0 + 8, :] = out
        vref[c0 : c0 + 8, :] = outw


def split(x):
    high = x.astype(jnp.bfloat16)
    low = (x - high.astype(F32)).astype(jnp.bfloat16)
    return high, low


def dot3(a, b, dims):
    d = functools.partial(lax.dot_general, dimension_numbers=dims, preferred_element_type=F32)
    return d(a[0], b[0]) + (d(a[0], b[1]) + d(a[1], b[0]))


def dot6(a, b, dims):
    return lax.dot_general(a, b, dims, precision=lax.Precision.HIGHEST, preferred_element_type=F32)


def thirds(x):
    high = x.astype(jnp.bfloat16)
    rest = x - high.astype(F32)
    mid = rest.astype(jnp.bfloat16)
    low = (rest - mid.astype(F32)).astype(jnp.bfloat16)
    return high, mid, low


def left6(x):
    h, m, l = thirds(x)
    return jnp.concatenate([h, m, h, m, h, l], axis=1)


def right6(x, axis):
    h, m, l = thirds(x)
    return jnp.concatenate([h, h, m, m, l, h], axis=axis)


def product(a, b, dims):
    return lax.dot_general(a, b, dims, preferred_element_type=F32)


def factor_lead(a, w, dblk, vblk, lleft, lright):
    n = LEAD
    blocks = n // B
    wide = 2 * B
    ri = lax.broadcasted_iota(jnp.int32, (B, B), 0)
    ci = lax.broadcasted_iota(jnp.int32, (B, B), 1)
    eye = jnp.where(ri == ci, 1.0, 0.0).astype(F32)
    wi = lax.broadcasted_iota(jnp.int32, (B, n), 0)
    wj = lax.broadcasted_iota(jnp.int32, (B, n), 1)
    for i in range(blocks):
        w[i * B : (i + 1) * B, :] = jnp.where(wi + i * B == wj, 1.0, 0.0)
    w[n:, :] = jnp.zeros((B, n), F32)
    a[0:n, n:] = jnp.zeros((n, B), F32)
    a[n:, :] = jnp.zeros((B, n + B), F32)

    def step(j, carry):
        o = pl.multiple_of(j * B, B)
        d = a[pl.ds(o, B), pl.ds(o, B)]
        dblk[...] = jnp.where(ri >= ci, d, d.T)
        vblk[...] = eye
        factor_block(dblk, vblk)
        a[pl.ds(o, B), pl.ds(o, B)] = jnp.where(ri <= ci, dblk[...], 0.0).T
        winv = vblk[...]
        wright = right6(winv, 1)
        wleft = left6(winv)
        pairs = (blocks - j) // 2

        def below(m):
            return pl.multiple_of(o + B + m * wide, B)

        def solve(m, c):
            r = below(m)
            solved = product(left6(a[pl.ds(r, wide), pl.ds(o, B)]), wright, NT)
            a[pl.ds(r, wide), pl.ds(o, B)] = solved
            lleft[pl.ds(r, wide), :] = left6(solved)
            lright[pl.ds(r, wide), :] = right6(solved, 1)
            return c

        lax.fori_loop(0, pairs, solve, 0)

        def reduce(k, c):
            at = pl.multiple_of(k * wide, wide)
            wrow = product(wleft, right6(w[pl.ds(o, B), pl.ds(at, wide)], 0), NN)
            w[pl.ds(o, B), pl.ds(at, wide)] = wrow
            right = right6(wrow, 0)

            def down(m, cc):
                r = below(m)
                w[pl.ds(r, wide), pl.ds(at, wide)] -= product(lleft[pl.ds(r, wide), :], right, NN)
                return cc

            lax.fori_loop(0, pairs, down, 0)
            return c

        lax.fori_loop(0, j // 2 + 1, reduce, 0)

        def update(k, c):
            s = below(k)
            right = lright[pl.ds(s, wide), :]

            def down(m, cc):
                r = below(m)
                a[pl.ds(r, wide), pl.ds(s, wide)] -= product(lleft[pl.ds(r, wide), :], right, NT)
                return cc

            lax.fori_loop(k, pairs, down, 0)
            return c

        lax.fori_loop(0, pairs, update, 0)
        return carry

    lax.fori_loop(0, blocks, step, 0)


def factor_kernel(lead_ref, strip_ref, solved_ref, shown_ref, a, w, dblk, vblk, lleft, lright):
    wide = lax.axis_index("wide")
    tall = lax.axis_index("tall")
    a[0:LEAD, 0:LEAD] = lead_ref[...]
    factor_lead(a, w, dblk, vblk, lleft, lright)
    shown_ref[...] = a[pl.ds(pl.multiple_of(tall * B, B), B), 0:LEAD]
    solved = dot6(strip_ref[...], w[0:LEAD, :], NT)
    cols = lax.broadcasted_iota(jnp.int32, solved.shape, 1)
    keep = (wide > 0) | ((tall >= PANEL // B) & (cols < PANEL))
    solved_ref[...] = jnp.where(keep, solved, 0.0)


def factor_and_solve(lead, strip):
    return pl.pallas_call(
        factor_kernel,
        out_shape=(jax.ShapeDtypeStruct((B, LEAD), F32),) * 2,
        in_specs=[vmem_spec()] * 2,
        out_specs=(vmem_spec(),) * 2,
        scratch_shapes=[
            pltpu.VMEM((PADDED, PADDED), F32),
            pltpu.VMEM((PADDED, LEAD), F32),
            pltpu.VMEM((B, B), F32),
            pltpu.VMEM((B, B), F32),
            pltpu.VMEM((PADDED, 6 * B), jnp.bfloat16),
            pltpu.VMEM((PADDED, 6 * B), jnp.bfloat16),
        ],
        compiler_params=params(),
        name="factor",
    )(lead, strip)


def share_kernel(mine_ref, rows_ref, cols_ref, send_sem, row_sem, col_sem, local_sem):
    w, t, z, x, c, h, y = place()
    side = neighbours()
    half = B // 2
    target = 2 * lax.rem(w, 8) + h
    quarter = w // 8
    pair = w // 2
    holder = h == c
    away = target != w
    barrier = pltpu.get_barrier_semaphore()
    extra = [(away, target)] + [(holder & (q * 8 + pair != w), q * 8 + pair) for q in range(2)]
    for partner in side.values():
        pl.semaphore_signal(barrier, inc=1, device_id=partner, device_id_type=MESH)
    for pred, k in extra:
        @pl.when(pred)
        def _():
            pl.semaphore_signal(barrier, inc=1, device_id=(k, t), device_id_type=MESH)
    peers = len(side)
    for pred, _ in extra:
        peers = peers + jnp.where(pred, 1, 0)
    pl.semaphore_wait(barrier, peers)
    sent = []
    count = [0]

    def copy_to(src, dst, sem, device):
        slot = count[0]
        count[0] += 1
        return pltpu.make_async_remote_copy(
            src_ref=src, dst_ref=dst, send_sem=send_sem.at[slot], recv_sem=sem,
            device_id=device, device_id_type=MESH,
        )

    def push(ref, sem, to):
        return copy_to(ref, ref, sem, side[to])

    def go(copy, pred=None):
        if pred is None:
            copy.start()
        else:
            @pl.when(pred)
            def _():
                copy.start()
        sent.append((pred, copy))

    def rpiece(k, n):
        return rows_ref.at[k, pl.ds(n * half, half), :]

    def cpiece(q, i, n):
        return cols_ref.at[q * 4 + i, pl.ds(n * half, half), :]

    def mpiece(n):
        return mine_ref.at[pl.ds(n * half, half), :]

    own = pltpu.make_async_copy(mine_ref, rows_ref.at[w], local_sem.at[0])
    own.start()
    kept = pltpu.make_async_copy(mine_ref, cols_ref.at[quarter * 4 + y], local_sem.at[1])

    @pl.when(jnp.logical_not(away))
    def _():
        kept.start()

    for n in range(2):
        go(copy_to(mpiece(n), cpiece(quarter, y, n), col_sem.at[quarter, y, n], (target, t)), away)
        for to in ("side", "up", "down", "core"):
            go(copy_to(mpiece(n), rpiece(w, n), row_sem.at[w, n], side[to]))

    @pl.when(jnp.logical_not(away))
    def _():
        kept.wait()

    beside = wide_at(z, 1 - x, c)
    for n in range(2):
        arrived(rpiece(beside, n), row_sem.at[beside, n])
        for to in ("up", "down", "core"):
            go(push(rpiece(beside, n), row_sem.at[beside, n], to))

    def take(q, n):
        @pl.when(jnp.logical_not(holder) | (q * 8 + pair != w))
        def _():
            arrived(cpiece(q, y, n), col_sem.at[q, y, n])

        go(push(cpiece(q, y, n), col_sem.at[q, y, n], "far"), holder)
        go(push(cpiece(q, y, n), col_sem.at[q, y, n], "north"))
        go(push(cpiece(q, y, n), col_sem.at[q, y, n], "south"))

    def next_rows(xx, n):
        for dz, to, part in ((-1, "up", 0), (1, "down", 1)):
            k = wide_at(z + dz, xx, c)
            arrived(rpiece(k, n), row_sem.at[k, n])
            if n == part:
                go(push(rpiece(k, n), row_sem.at[k, n], to))
            go(push(rpiece(k, n), row_sem.at[k, n], "core"))

    for q in range(2):
        take(q, 0)
    for n in range(2):
        next_rows(x, n)
    for q in range(2):
        take(q, 1)
    for n in range(2):
        next_rows(1 - x, n)
    for q in range(2):
        for n in range(2):
            for dy, to, part in ((-1, "north", 0), (1, "south", 1)):
                i = lax.rem(y + dy + 4, 4)
                arrived(cpiece(q, i, n), col_sem.at[q, i, n])
                if n == part:
                    go(push(cpiece(q, i, n), col_sem.at[q, i, n], to))
    for xx in (x, 1 - x):
        for n in range(2):
            k = wide_at(z + 2, xx, c)
            arrived(rpiece(k, n), row_sem.at[k, n])
            go(push(rpiece(k, n), row_sem.at[k, n], "core"))
    for q in range(2):
        for n in range(2):
            i = lax.rem(y + 2, 4)
            arrived(cpiece(q, i, n), col_sem.at[q, i, n])
    for zz in (z, z - 1, z + 1, z + 2):
        for xx in (x, 1 - x):
            k = wide_at(zz, xx, 1 - c)
            for n in range(2):
                arrived(rpiece(k, n), row_sem.at[k, n])
    own.wait()
    for pred, copy in sent:
        if pred is None:
            copy.wait_send()
        else:
            @pl.when(pred)
            def _():
                copy.wait_send()


def share_solved(mine):
    return pl.pallas_call(
        share_kernel,
        out_shape=(
            jax.ShapeDtypeStruct((16, B, LEAD), F32),
            jax.ShapeDtypeStruct((8, B, LEAD), F32),
        ),
        in_specs=[vmem_spec()],
        out_specs=(any_spec(), any_spec()),
        scratch_shapes=[
            pltpu.SemaphoreType.DMA((64,)),
            pltpu.SemaphoreType.DMA((16, 2)),
            pltpu.SemaphoreType.DMA((2, 4, 2)),
            pltpu.SemaphoreType.DMA((2,)),
        ],
        compiler_params=params(collective_id=1, has_side_effects=True),
        name="share_solved",
    )(mine)


def update_kernel(front_ref, rows_ref, cols_ref, shown_ref, out_ref, high, low):
    step = pl.program_id(0)
    wide = lax.axis_index("wide")
    tall = lax.axis_index("tall")

    @pl.when(step == 0)
    def _():
        for i in range(LEAD // B):
            h, l = split(cols_ref[i * B : (i + 1) * B, :])
            high[i * B : (i + 1) * B, :] = h
            low[i * B : (i + 1) * B, :] = l

    mine = rows_ref[...]
    change = dot3(split(mine), (high[...], low[...]), NT)
    out = front_ref[...] - change
    out_ref[...] = out
    for p in range(2):
        @pl.when(wide == p)
        def _():
            out_ref[:, 0:PANEL] = mine[:, p * PANEL : (p + 1) * PANEL]

            @pl.when(step == 0)
            def _():
                r = lax.broadcasted_iota(jnp.int32, (B, PANEL), 0) + tall * B
                c = lax.broadcasted_iota(jnp.int32, (B, PANEL), 1) + p * PANEL
                out_ref[0:B, 0:PANEL] = jnp.where(
                    r >= c, shown_ref[:, p * PANEL : (p + 1) * PANEL], out[0:B, 0:PANEL]
                )


def update(front, rows, cols, shown):
    total, width = front.shape
    chunk = 256
    return pl.pallas_call(
        update_kernel,
        grid=(total // chunk,),
        out_shape=jax.ShapeDtypeStruct(front.shape, F32),
        in_specs=[
            pl.BlockSpec((chunk, width), lambda i: (i, 0)),
            pl.BlockSpec((chunk, LEAD), lambda i: (i, 0)),
            pl.BlockSpec((width, LEAD), lambda i: (0, 0)),
            pl.BlockSpec((B, LEAD), lambda i: (0, 0)),
        ],
        out_specs=pl.BlockSpec((chunk, width), lambda i: (i, 0)),
        scratch_shapes=[pltpu.VMEM((width, LEAD), jnp.bfloat16)] * 2,
        compiler_params=params(),
        name="update",
    )(front, rows, cols, shown)


def body(initial, child_tiles, child_targets):
    wides = lax.axis_size("wide")
    cols = share_cols(child_targets[:, 1], lax.axis_size("tall"))
    tiles = lax.all_to_all(child_tiles, "tall", split_axis=0, concat_axis=0, tiled=True)
    slab, strip = add_tiles(initial, tiles, cols, wides)
    lead = share_lead(strip)
    front = lax.all_to_all(slab, "wide", split_axis=0, concat_axis=0, tiled=True)
    solved, shown = factor_and_solve(lead.reshape(LEAD, LEAD), strip)
    rows, columns = share_solved(solved)
    front = front.reshape(-1, slab.shape[2])
    return update(front, rows.reshape(-1, LEAD), columns.reshape(-1, LEAD), shown)


def solution(mesh):
    return jax.shard_map(
        body,
        mesh=mesh,
        in_specs=(
            P(("wide", "tall"), None),
            P(("wide", "tall"), None, None),
            P(("wide", "tall"), None),
        ),
        out_specs=P("tall", "wide"),
        check_vma=False,
    )
```

```python
import functools

import jax
import jax.numpy as jnp
from jax import lax
from jax.experimental import pallas as pl
from jax.experimental.pallas import tpu as pltpu
from jax.sharding import PartitionSpec as P

PANEL = 512
LEAD = 1024
B = 128
ROWS = LEAD + 2 * B
COLS = LEAD + B
MESH = pl.DeviceIdType.MESH
NT = (((1,), (1,)), ((), ()))
VMEM_LIMIT = 60 * 1024 * 1024
F32 = jnp.float32


def vmem_spec():
    return pl.BlockSpec(memory_space=pltpu.VMEM)


def any_spec():
    return pl.BlockSpec(memory_space=pl.ANY)


def params(**more):
    return pltpu.CompilerParams(vmem_limit_bytes=VMEM_LIMIT, **more)


def add_kernel(cols_ref, initial_ref, tiles_ref, out_ref, strip_ref, acc, tiles, sem_in, sem_tile, sem_out, sem_strip):
    wides = acc.shape[0]
    halves = acc.shape[2] // PANEL
    count = tiles.shape[0]
    loads = []
    for q in range(halves):
        for w in range(wides):
            at = (q * wides + w) * PANEL
            loads.append(
                pltpu.make_async_copy(
                    initial_ref.at[:, at : at + PANEL],
                    acc.at[w, :, q * PANEL : (q + 1) * PANEL],
                    sem_in.at[q * wides + w],
                )
            )
    tile_load = pltpu.make_async_copy(tiles_ref, tiles, sem_tile)
    for load in loads:
        load.start()
    tile_load.start()
    for load in loads:
        load.wait()
    tile_load.wait()
    per_panel = PANEL // B

    def add(n, carry):
        col = cols_ref[n]
        block = col // per_panel
        at = pl.multiple_of((block // wides) * PANEL + (col % per_panel) * B, B)
        acc[block % wides, :, pl.ds(at, B)] += tiles[n]
        return carry

    lax.fori_loop(0, count, add, 0)
    stores = [
        pltpu.make_async_copy(acc.at[0, :, 0:PANEL], strip_ref.at[:, 0:PANEL], sem_strip.at[0]),
        pltpu.make_async_copy(acc.at[1, :, 0:PANEL], strip_ref.at[:, PANEL:LEAD], sem_strip.at[1]),
    ]
    for w in range(wides):
        stores.append(pltpu.make_async_copy(acc.at[w], out_ref.at[w], sem_out.at[w]))
    for store in stores:
        store.start()
    for store in stores:
        store.wait()


def add_tiles(initial, tiles, cols, wides):
    rows, order = initial.shape
    count = tiles.shape[0]
    width = order // wides
    return pl.pallas_call(
        add_kernel,
        grid_spec=pltpu.PrefetchScalarGridSpec(
            num_scalar_prefetch=1,
            grid=(1,),
            in_specs=[any_spec(), any_spec()],
            out_specs=[any_spec(), any_spec()],
            scratch_shapes=[
                pltpu.VMEM((wides, rows, width), F32),
                pltpu.VMEM((count, B, B), F32),
                pltpu.SemaphoreType.DMA((order // PANEL,)),
                pltpu.SemaphoreType.DMA,
                pltpu.SemaphoreType.DMA((wides,)),
                pltpu.SemaphoreType.DMA((2,)),
            ],
        ),
        out_shape=[
            jax.ShapeDtypeStruct((wides, rows, width), F32),
            jax.ShapeDtypeStruct((rows, LEAD), F32),
        ],
        compiler_params=params(),
        name="add_tiles",
    )(cols, initial, tiles)


def place():
    w = lax.axis_index("wide")
    t = lax.axis_index("tall")
    z, x, c = w // 4, (w // 2) % 2, w % 2
    h, y = t // 4, t % 4
    return w, t, z, x, c, h, y


def wide_at(z, x, c):
    return lax.rem(z + 4, 4) * 4 + x * 2 + c


def tall_at(h, y):
    return h * 4 + lax.rem(y + 4, 4)


def neighbours():
    w, t, z, x, c, h, y = place()
    return {
        "up": (wide_at(z + 1, x, c), t),
        "down": (wide_at(z - 1, x, c), t),
        "side": (wide_at(z, 1 - x, c), t),
        "core": (wide_at(z, x, 1 - c), t),
        "far": (w, tall_at(1 - h, y)),
        "north": (w, tall_at(h, y + 1)),
        "south": (w, tall_at(h, y - 1)),
    }


def greet(partners):
    barrier = pltpu.get_barrier_semaphore()
    for partner in partners:
        pl.semaphore_signal(barrier, inc=1, device_id=partner, device_id_type=MESH)
    pl.semaphore_wait(barrier, len(partners))


def send(src, dst, send_sem, recv_sem, partner):
    copy = pltpu.make_async_remote_copy(
        src_ref=src, dst_ref=dst, send_sem=send_sem, recv_sem=recv_sem,
        device_id=partner, device_id_type=MESH,
    )
    copy.start()
    return copy


def arrived(ref, sem):
    pltpu.make_async_copy(ref, ref, sem).wait()


def cols_kernel(src_ref, out_ref, send_sem, recv_sem, local_sem):
    w, t = lax.axis_index("wide"), lax.axis_index("tall")
    talls = src_ref.shape[0]
    greet([(w, lax.rem(t + d, talls)) for d in range(1, talls)])
    own = pltpu.make_async_copy(src_ref.at[t], out_ref.at[t], local_sem)
    own.start()
    sent = []
    for d in range(1, talls):
        to = lax.rem(t + d, talls)
        sent.append(send(src_ref.at[to], out_ref.at[t], send_sem.at[d], recv_sem.at[t], (w, to)))
    for d in range(1, talls):
        source = lax.rem(t + talls - d, talls)
        arrived(out_ref.at[source], recv_sem.at[source])
    own.wait()
    for copy in sent:
        copy.wait_send()


def share_cols(cols, talls):
    each = cols.shape[0] // talls
    padded = jnp.pad(cols.reshape(talls, 1, each), ((0, 0), (0, 7), (0, B - each)))
    got = pl.pallas_call(
        cols_kernel,
        out_shape=jax.ShapeDtypeStruct(padded.shape, padded.dtype),
        in_specs=[vmem_spec()],
        out_specs=vmem_spec(),
        scratch_shapes=[
            pltpu.SemaphoreType.DMA((talls,)),
            pltpu.SemaphoreType.DMA((talls,)),
            pltpu.SemaphoreType.DMA,
        ],
        compiler_params=params(collective_id=2, has_side_effects=True),
        name="share_cols",
    )(padded)
    return got[:, 0, :each].reshape(-1)


CHUNKS = 4


def lead_kernel(strip_ref, lead_ref, send_sem, recv_sem, core_sem, local_sem):
    w, t, z, x, c, h, y = place()
    side = neighbours()
    greet(list(side.values()))
    half = B // 2
    rows = half // CHUNKS
    sent = []

    def piece(block, core, n):
        return lead_ref.at[block, pl.ds(core * half + n * rows, rows), :]

    def push(block, core, n, to, sem, slot):
        copy = pltpu.make_async_remote_copy(
            src_ref=piece(block, core, n), dst_ref=piece(block, core, n),
            send_sem=send_sem.at[slot, n], recv_sem=sem.at[block, n],
            device_id=side[to], device_id_type=MESH,
        )
        return copy

    def go(pred, copy):
        if pred is None:
            copy.start()
            sent.append((None, copy))
        else:
            @pl.when(pred)
            def _():
                copy.start()
            sent.append((pred, copy))

    other = 1 - c
    far = tall_at(1 - h, y)
    is_root = w == 0
    own = pltpu.make_async_copy(strip_ref, lead_ref.at[t], local_sem)

    @pl.when(is_root)
    def _():
        own.start()
        own.wait()

    for n in range(CHUNKS):
        go(is_root, push(t, 1, n, "core", recv_sem, 0))
    for n in range(CHUNKS):
        @pl.when(w != 0)
        def _():
            arrived(piece(t, c, n), recv_sem.at[t, n])
        base = x == 0
        go(base & (z == 0), push(t, c, n, "up", recv_sem, 1))
        go(base & (z == 0), push(t, c, n, "down", recv_sem, 2))
        if n % 2 == 0:
            go(base & (z == 1), push(t, c, n, "up", recv_sem, 1))
        else:
            go(base & (z == 3), push(t, c, n, "down", recv_sem, 2))
        go(base, push(t, c, n, "side", recv_sem, 3))
        go(None, push(t, c, n, "far", recv_sem, 4))
        go(None, push(t, c, n, "north", recv_sem, 5))
        go(None, push(t, c, n, "south", recv_sem, 6))
        go(w > 1, push(t, c, n, "core", core_sem, 0))
        go(w == 0, push(t, c, n, "core", core_sem, 7))
    for n in range(CHUNKS):
        arrived(piece(far, c, n), recv_sem.at[far, n])
        go(None, push(far, c, n, "north", recv_sem, 8))
        go(None, push(far, c, n, "south", recv_sem, 9))
        go(None, push(far, c, n, "core", core_sem, 10))
    for n in range(CHUNKS):
        slot = 11
        for hh in (h, 1 - h):
            for step, to in ((-1, "north"), (1, "south")):
                block = tall_at(hh, y + step)
                arrived(piece(block, c, n), recv_sem.at[block, n])
                if n % 2 == (0 if to == "north" else 1):
                    go(None, push(block, c, n, to, recv_sem, slot))
                go(None, push(block, c, n, "core", core_sem, slot + 1))
                slot += 2
    for n in range(CHUNKS):
        for i, hh in enumerate((h, 1 - h)):
            block = tall_at(hh, y + 2)
            arrived(piece(block, c, n), recv_sem.at[block, n])
            go(None, push(block, c, n, "core", core_sem, 19 + i))
    for n in range(CHUNKS):
        for block in range(8):
            @pl.when((w != 0) | (block != t))
            def _():
                arrived(piece(block, other, n), core_sem.at[block, n])
    for pred, copy in sent:
        if pred is None:
            copy.wait_send()
        else:
            @pl.when(pred)
            def _():
                copy.wait_send()


def share_lead(strip):
    return pl.pallas_call(
        lead_kernel,
        out_shape=jax.ShapeDtypeStruct((LEAD // B, B, LEAD), F32),
        in_specs=[vmem_spec()],
        out_specs=vmem_spec(),
        scratch_shapes=[
            pltpu.SemaphoreType.DMA((21, CHUNKS)),
            pltpu.SemaphoreType.DMA((8, CHUNKS)),
            pltpu.SemaphoreType.DMA((8, CHUNKS)),
            pltpu.SemaphoreType.DMA,
        ],
        compiler_params=params(collective_id=0, has_side_effects=True),
        name="share_lead",
    )(strip)


def lane(x, c):
    return jnp.broadcast_to(x[:, c : c + 1], (x.shape[0], B))


def row(x, r):
    return jnp.broadcast_to(x[r : r + 1, :], (8, x.shape[1]))


def factor_block(dref, vref):
    for m in range(B // 8):
        c0 = 8 * m
        p = dref[c0 : c0 + 8, :]
        wp = vref[c0 : c0 + 8, :]
        q = [lane(p, c0 + k) for k in range(8)]
        s = [[row(q[j], i) if j <= i else None for j in range(8)] for i in range(8)]
        f = [[None] * 8 for _ in range(8)]
        dinv = [None] * 8
        for j in range(8):
            dinv[j] = 1.0 / s[j][j]
            for i in range(j + 1, 8):
                f[i][j] = s[i][j] * dinv[j]
            for i in range(j + 1, 8):
                for k in range(j + 1, i + 1):
                    s[i][k] = s[i][k] - f[i][j] * s[k][j]
        r = [row(p, j) for j in range(8)]
        rw = [row(wp, j) for j in range(8)]
        for j in range(8):
            for i in range(j + 1, 8):
                r[i] = r[i] - f[i][j] * r[j]
                rw[i] = rw[i] - f[i][j] * rw[j]
        u = [r[j] * dinv[j] for j in range(8)]
        uw = [rw[j] * dinv[j] for j in range(8)]
        for j in range(7, 0, -1):
            for i in range(j):
                u[i] = u[i] - f[j][i] * u[j]
                uw[i] = uw[i] - f[j][i] * uw[j]
        for v in range(m + 1, B // 8):
            rows = dref[8 * v : 8 * v + 8, :]
            wrows = vref[8 * v : 8 * v + 8, :]
            acc = accw = None
            for j in range(8):
                c = lane(rows, c0 + j)
                acc = c * u[j] if acc is None else acc + c * u[j]
                accw = c * uw[j] if accw is None else accw + c * uw[j]
            dref[8 * v : 8 * v + 8, :] = rows - acc
            vref[8 * v : 8 * v + 8, :] = wrows - accw
        sub = lax.broadcasted_iota(jnp.int32, (8, B), 0)
        out = outw = None
        for j in range(8):
            scale = lax.rsqrt(s[j][j])
            a, b = r[j] * scale, rw[j] * scale
            out = a if out is None else jnp.where(sub == j, a, out)
            outw = b if outw is None else jnp.where(sub == j, b, outw)
        dref[c0 : c0 + 8, :] = out
        vref[c0 : c0 + 8, :] = outw


def split(x):
    high = x.astype(jnp.bfloat16)
    low = (x - high.astype(F32)).astype(jnp.bfloat16)
    return high, low


def dot3(a, b, dims):
    d = functools.partial(lax.dot_general, dimension_numbers=dims, preferred_element_type=F32)
    return d(a[0], b[0]) + (d(a[0], b[1]) + d(a[1], b[0]))


def thirds(x):
    high = x.astype(jnp.bfloat16)
    rest = x - high.astype(F32)
    mid = rest.astype(jnp.bfloat16)
    low = (rest - mid.astype(F32)).astype(jnp.bfloat16)
    return high, mid, low


def left6(x):
    h, m, l = thirds(x)
    return jnp.concatenate([h, m, h, m, h, l], axis=1)


def right6(x, axis):
    h, m, l = thirds(x)
    return jnp.concatenate([h, h, m, m, l, h], axis=axis)


def product(a, b, dims):
    return lax.dot_general(a, b, dims, preferred_element_type=F32)


def factor_lead(a, dblk, vblk, lleft, lright):
    blocks = LEAD // B
    wide = 2 * B
    ri = lax.broadcasted_iota(jnp.int32, (B, B), 0)
    ci = lax.broadcasted_iota(jnp.int32, (B, B), 1)
    eye = jnp.where(ri == ci, 1.0, 0.0).astype(F32)
    a[LEAD + B :, :] = jnp.zeros((ROWS - LEAD - B, COLS), F32)
    a[0 : LEAD + B, LEAD:] = jnp.zeros((LEAD + B, COLS - LEAD), F32)

    def step(j, carry):
        o = pl.multiple_of(j * B, B)
        d = a[pl.ds(o, B), pl.ds(o, B)]
        dblk[...] = jnp.where(ri >= ci, d, d.T)
        vblk[...] = eye
        factor_block(dblk, vblk)
        a[pl.ds(o, B), pl.ds(o, B)] = jnp.where(ri <= ci, dblk[...], 0.0).T
        inverse = right6(vblk[...], 1)
        row_pairs = (blocks - j + 1) // 2
        col_pairs = (blocks - j) // 2

        def below(m):
            return pl.multiple_of(o + B + m * wide, B)

        def solve(m, c):
            r = below(m)
            solved = product(left6(a[pl.ds(r, wide), pl.ds(o, B)]), inverse, NT)
            a[pl.ds(r, wide), pl.ds(o, B)] = solved
            lleft[pl.ds(r, wide), :] = left6(solved)
            lright[pl.ds(r, wide), :] = right6(solved, 1)
            return c

        lax.fori_loop(0, row_pairs, solve, 0)

        def update(k, c):
            s = below(k)
            right = lright[pl.ds(s, wide), :]

            def down(m, cc):
                r = below(m)
                a[pl.ds(r, wide), pl.ds(s, wide)] -= product(lleft[pl.ds(r, wide), :], right, NT)
                return cc

            lax.fori_loop(k, row_pairs, down, 0)
            return c

        lax.fori_loop(0, col_pairs, update, 0)
        return carry

    lax.fori_loop(0, blocks, step, 0)


def factor_kernel(lead_ref, strip_ref, solved_ref, shown_ref, a, dblk, vblk, lleft, lright):
    wide = lax.axis_index("wide")
    tall = lax.axis_index("tall")
    a[0:LEAD, 0:LEAD] = lead_ref[...]
    a[LEAD : LEAD + B, 0:LEAD] = strip_ref[...]
    factor_lead(a, dblk, vblk, lleft, lright)
    shown_ref[...] = a[pl.ds(pl.multiple_of(tall * B, B), B), 0:LEAD]
    solved = a[LEAD : LEAD + B, 0:LEAD]
    cols = lax.broadcasted_iota(jnp.int32, solved.shape, 1)
    keep = (wide > 0) | ((tall >= PANEL // B) & (cols < PANEL))
    solved_ref[...] = jnp.where(keep, solved, 0.0)


def factor_and_solve(lead, strip):
    return pl.pallas_call(
        factor_kernel,
        out_shape=(jax.ShapeDtypeStruct((B, LEAD), F32),) * 2,
        in_specs=[vmem_spec()] * 2,
        out_specs=(vmem_spec(),) * 2,
        scratch_shapes=[
            pltpu.VMEM((ROWS, COLS), F32),
            pltpu.VMEM((B, B), F32),
            pltpu.VMEM((B, B), F32),
            pltpu.VMEM((ROWS, 6 * B), jnp.bfloat16),
            pltpu.VMEM((ROWS, 6 * B), jnp.bfloat16),
        ],
        compiler_params=params(),
        name="factor",
    )(lead, strip)


def share_kernel(mine_ref, rows_ref, cols_ref, send_sem, row_sem, col_sem, local_sem):
    w, t, z, x, c, h, y = place()
    side = neighbours()
    half = B // 2
    target = 2 * lax.rem(w, 8) + h
    quarter = w // 8
    pair = w // 2
    holder = h == c
    away = target != w
    barrier = pltpu.get_barrier_semaphore()
    extra = [(away, target)] + [(holder & (q * 8 + pair != w), q * 8 + pair) for q in range(2)]
    for partner in side.values():
        pl.semaphore_signal(barrier, inc=1, device_id=partner, device_id_type=MESH)
    for pred, k in extra:
        @pl.when(pred)
        def _():
            pl.semaphore_signal(barrier, inc=1, device_id=(k, t), device_id_type=MESH)
    peers = len(side)
    for pred, _ in extra:
        peers = peers + jnp.where(pred, 1, 0)
    pl.semaphore_wait(barrier, peers)
    sent = []
    count = [0]

    def copy_to(src, dst, sem, device):
        slot = count[0]
        count[0] += 1
        return pltpu.make_async_remote_copy(
            src_ref=src, dst_ref=dst, send_sem=send_sem.at[slot], recv_sem=sem,
            device_id=device, device_id_type=MESH,
        )

    def push(ref, sem, to):
        return copy_to(ref, ref, sem, side[to])

    def go(copy, pred=None):
        if pred is None:
            copy.start()
        else:
            @pl.when(pred)
            def _():
                copy.start()
        sent.append((pred, copy))

    def rpiece(k, n):
        return rows_ref.at[k, pl.ds(n * half, half), :]

    def cpiece(q, i, n):
        return cols_ref.at[q * 4 + i, pl.ds(n * half, half), :]

    def mpiece(n):
        return mine_ref.at[pl.ds(n * half, half), :]

    own = pltpu.make_async_copy(mine_ref, rows_ref.at[w], local_sem.at[0])
    own.start()
    kept = pltpu.make_async_copy(mine_ref, cols_ref.at[quarter * 4 + y], local_sem.at[1])

    @pl.when(jnp.logical_not(away))
    def _():
        kept.start()

    for n in range(2):
        go(copy_to(mpiece(n), cpiece(quarter, y, n), col_sem.at[quarter, y, n], (target, t)), away)
        for to in ("side", "up", "down", "core"):
            go(copy_to(mpiece(n), rpiece(w, n), row_sem.at[w, n], side[to]))

    @pl.when(jnp.logical_not(away))
    def _():
        kept.wait()

    beside = wide_at(z, 1 - x, c)
    for n in range(2):
        arrived(rpiece(beside, n), row_sem.at[beside, n])
        for to in ("up", "down", "core"):
            go(push(rpiece(beside, n), row_sem.at[beside, n], to))

    def take(q, n):
        @pl.when(jnp.logical_not(holder) | (q * 8 + pair != w))
        def _():
            arrived(cpiece(q, y, n), col_sem.at[q, y, n])

        go(push(cpiece(q, y, n), col_sem.at[q, y, n], "far"), holder)
        go(push(cpiece(q, y, n), col_sem.at[q, y, n], "north"))
        go(push(cpiece(q, y, n), col_sem.at[q, y, n], "south"))

    def next_rows(xx, n):
        for dz, to, part in ((-1, "up", 0), (1, "down", 1)):
            k = wide_at(z + dz, xx, c)
            arrived(rpiece(k, n), row_sem.at[k, n])
            if n == part:
                go(push(rpiece(k, n), row_sem.at[k, n], to))
            go(push(rpiece(k, n), row_sem.at[k, n], "core"))

    for q in range(2):
        take(q, 0)
    for n in range(2):
        next_rows(x, n)
    for q in range(2):
        take(q, 1)
    for n in range(2):
        next_rows(1 - x, n)
    for q in range(2):
        for n in range(2):
            for dy, to, part in ((-1, "north", 0), (1, "south", 1)):
                i = lax.rem(y + dy + 4, 4)
                arrived(cpiece(q, i, n), col_sem.at[q, i, n])
                if n == part:
                    go(push(cpiece(q, i, n), col_sem.at[q, i, n], to))
    for xx in (x, 1 - x):
        for n in range(2):
            k = wide_at(z + 2, xx, c)
            arrived(rpiece(k, n), row_sem.at[k, n])
            go(push(rpiece(k, n), row_sem.at[k, n], "core"))
    for q in range(2):
        for n in range(2):
            i = lax.rem(y + 2, 4)
            arrived(cpiece(q, i, n), col_sem.at[q, i, n])
    for zz in (z, z - 1, z + 1, z + 2):
        for xx in (x, 1 - x):
            k = wide_at(zz, xx, 1 - c)
            for n in range(2):
                arrived(rpiece(k, n), row_sem.at[k, n])
    own.wait()
    for pred, copy in sent:
        if pred is None:
            copy.wait_send()
        else:
            @pl.when(pred)
            def _():
                copy.wait_send()


def share_solved(mine):
    return pl.pallas_call(
        share_kernel,
        out_shape=(
            jax.ShapeDtypeStruct((16, B, LEAD), F32),
            jax.ShapeDtypeStruct((8, B, LEAD), F32),
        ),
        in_specs=[vmem_spec()],
        out_specs=(any_spec(), any_spec()),
        scratch_shapes=[
            pltpu.SemaphoreType.DMA((64,)),
            pltpu.SemaphoreType.DMA((16, 2)),
            pltpu.SemaphoreType.DMA((2, 4, 2)),
            pltpu.SemaphoreType.DMA((2,)),
        ],
        compiler_params=params(collective_id=1, has_side_effects=True),
        name="share_solved",
    )(mine)


def update_kernel(front_ref, rows_ref, cols_ref, shown_ref, out_ref, high, low):
    step = pl.program_id(0)
    wide = lax.axis_index("wide")
    tall = lax.axis_index("tall")

    @pl.when(step == 0)
    def _():
        for i in range(LEAD // B):
            h, l = split(cols_ref[i * B : (i + 1) * B, :])
            high[i * B : (i + 1) * B, :] = h
            low[i * B : (i + 1) * B, :] = l

    mine = rows_ref[...]
    change = dot3(split(mine), (high[...], low[...]), NT)
    out = front_ref[...] - change
    out_ref[...] = out
    for p in range(2):
        @pl.when(wide == p)
        def _():
            out_ref[:, 0:PANEL] = mine[:, p * PANEL : (p + 1) * PANEL]

            @pl.when(step == 0)
            def _():
                r = lax.broadcasted_iota(jnp.int32, (B, PANEL), 0) + tall * B
                c = lax.broadcasted_iota(jnp.int32, (B, PANEL), 1) + p * PANEL
                out_ref[0:B, 0:PANEL] = jnp.where(
                    r >= c, shown_ref[:, p * PANEL : (p + 1) * PANEL], out[0:B, 0:PANEL]
                )


def update(front, rows, cols, shown):
    total, width = front.shape
    chunk = 256
    return pl.pallas_call(
        update_kernel,
        grid=(total // chunk,),
        out_shape=jax.ShapeDtypeStruct(front.shape, F32),
        in_specs=[
            pl.BlockSpec((chunk, width), lambda i: (i, 0)),
            pl.BlockSpec((chunk, LEAD), lambda i: (i, 0)),
            pl.BlockSpec((width, LEAD), lambda i: (0, 0)),
            pl.BlockSpec((B, LEAD), lambda i: (0, 0)),
        ],
        out_specs=pl.BlockSpec((chunk, width), lambda i: (i, 0)),
        scratch_shapes=[pltpu.VMEM((width, LEAD), jnp.bfloat16)] * 2,
        compiler_params=params(),
        name="update",
    )(front, rows, cols, shown)


def body(initial, child_tiles, child_targets):
    wides = lax.axis_size("wide")
    cols = share_cols(child_targets[:, 1], lax.axis_size("tall"))
    tiles = lax.all_to_all(child_tiles, "tall", split_axis=0, concat_axis=0, tiled=True)
    slab, strip = add_tiles(initial, tiles, cols, wides)
    lead = share_lead(strip)
    slab, lead = lax.optimization_barrier((slab, lead))
    front = lax.all_to_all(slab, "wide", split_axis=0, concat_axis=0, tiled=True)
    solved, shown = factor_and_solve(lead.reshape(LEAD, LEAD), strip)
    rows, columns = share_solved(solved)
    front = front.reshape(-1, slab.shape[2])
    return update(front, rows.reshape(-1, LEAD), columns.reshape(-1, LEAD), shown)


def solution(mesh):
    return jax.shard_map(
        body,
        mesh=mesh,
        in_specs=(
            P(("wide", "tall"), None),
            P(("wide", "tall"), None, None),
            P(("wide", "tall"), None),
        ),
        out_specs=P("tall", "wide"),
        check_vma=False,
    )
```
